512 devices in a mesh: tm: 8 (over x, core), pair: 64 (over z, y).
Axes of the slice: x: 4, y: 4, z: 16, core: 2. Of those that a mesh axis runs over, the one named last changes fastest.
Arguments:
- traces: float32 [16, 8192, 1024], P('tm', 'pair'), may hold values from -6 to 6
- owner: int32 [64], replicated, may hold values from 0 to 63, each once
- tiles: int32 [192, 2], P('pair'), may hold values from 0 to 63, as said below
- counts: int32 [64], P('pair'), may hold values from 1 to 3, as said below
Outputs:
- stacks: float32 [192, 128, 16384], P('pair', None, 'tm')
The draws below stay inside these ranges and needn't reach their ends.
Inputs may be any that keep to these rules, and one draw needn't show every extreme that they name: `tiles`: each row names fiber blocks a <= b with b - a at most 6. `counts`: the first that many of an index's 3 slots are live; some index has all 3 live.
All inputs are finite; a program needn't handle non-finite values.
Results may differ from the reference program's by a relative error of at most 0.0038.
Values may be sent and summed in bfloat16 or wider, within the bound.
A program may use at most 64 MiB of HBM per device.

```python
import math
import jax
import jax.numpy as jnp
from jax import lax

BLOCK = 128
NT = 1024
NF = 128
LOW_BIN = 8
LAGS = 128
REACH = 6
PMAX = 3
NBLK = 64
CHANNELS = 8192
SEGMENTS = 16
SLOTS = 192


def draw_tiles(key, part):
    first = jax.random.randint(jax.random.fold_in(key, 11), (SLOTS, 1), 0, NBLK)
    offset = jax.random.randint(jax.random.fold_in(key, 12), (SLOTS, 1), 0, REACH + 1)
    second = jnp.minimum(first + offset, NBLK - 1)
    return jnp.concatenate([first, second], axis=1).astype(jnp.int32)


def draw_counts(key, part):
    base = jax.random.randint(jax.random.fold_in(key, 21), (NBLK,), 1, PMAX + 1)
    fullest = jax.random.randint(jax.random.fold_in(key, 22), (), 0, NBLK)
    return jnp.where(jnp.arange(NBLK) == fullest, PMAX, base).astype(jnp.int32)


def block_levels(stream_key, dims, shards, low, largest):
    def one(dim, blocks):
        steps = jax.random.uniform(jax.random.fold_in(jax.random.fold_in(stream_key, 6), dim), (blocks,), jnp.float32, low / len(shards), largest / len(shards))
        return jnp.repeat(jnp.exp(steps), dims[dim] // blocks).reshape((-1,) + (1,) * (len(dims) - dim - 1))

    loudness = one(*shards[0])
    for cut in shards[1:]:
        loudness = loudness * one(*cut)
    return loudness


def normal_values(key, shape, spread, bound, shards=(), kind=jnp.bfloat16):
    factor_of = block_levels(key, shape, shards, -0.22, 0.18) if shards else 1.0
    array = jax.random.normal(key, shape, jnp.float32) * spread * factor_of
    return jnp.minimum(jnp.maximum(array, -bound), bound).astype(kind)


def setup_inputs(seed: int = 0) -> dict:
    key_of = jax.random.split(jax.random.key(seed), 5)
    return {
        "traces": normal_values(key_of[0], (SEGMENTS, CHANNELS, NT), 1.0, 6.0, ((0, 8), (1, 64)), jnp.float32),
        "owner": jax.random.permutation(key_of[1], NBLK).astype(jnp.int32),
        "tiles": draw_tiles(jax.random.fold_in(key_of[4], 71), 0),
        "counts": draw_counts(jax.random.fold_in(key_of[4], 71), 0),
    }


def forward_table():
    samples = jnp.arange(NT, dtype=jnp.int32)
    bins = LOW_BIN + jnp.arange(NF, dtype=jnp.int32)
    phase = samples[:, None] * bins[None, :] % NT
    angle = phase.astype(jnp.float32) * (2.0 * math.pi / NT)
    return jnp.concatenate([jnp.cos(angle), -jnp.sin(angle)], axis=1)

def inverse_table():
    shifts = jnp.arange(LAGS, dtype=jnp.int32) - LAGS // 2
    bins = LOW_BIN + jnp.arange(NF, dtype=jnp.int32)
    phase = jnp.mod(shifts[:, None] * bins[None, :], NT)
    angle = phase.astype(jnp.float32) * (2.0 * math.pi / NT)
    return (jnp.cos(angle), -jnp.sin(angle))

def window_sum(values):
    widths = [(0, 0)] * (values.ndim - 1) + [(2, 2)]
    padded = jnp.pad(values, widths)
    total = padded[..., 0:NF]
    for offset in range(1, 5):
        total = total + padded[..., offset:offset + NF]
    return total

def whiten(spectrum):
    real_part = spectrum[..., :NF]
    imag_part = spectrum[..., NF:]
    power = real_part * real_part + imag_part * imag_part
    counted = window_sum(jnp.ones((NF,), jnp.float32))
    smooth = window_sum(power) / counted
    level = lax.optimization_barrier(jnp.mean(power, axis=-1, keepdims=True))
    factor = lax.rsqrt(smooth + 0.05 * level + 1e-06)
    return jnp.concatenate([real_part * factor, imag_part * factor], axis=-1).astype(jnp.bfloat16)

def reference(traces, owner, tiles, counts):
    rows = traces.reshape(SEGMENTS * CHANNELS, NT)
    spectrum = jnp.dot(rows, forward_table(), precision=lax.Precision.HIGHEST)
    white = whiten(spectrum).reshape(SEGMENTS, NBLK, BLOCK, 2 * NF)
    onehot = tiles[:, :, None] == jnp.arange(NBLK, dtype=jnp.int32)[None, None, :]
    stored = lax.optimization_barrier(jnp.sum(jnp.where(onehot, owner[None, None, :], 0), axis=2)).astype(jnp.int32)
    slot_rank = jnp.arange(SLOTS, dtype=jnp.int32) % PMAX
    holder = jnp.arange(SLOTS, dtype=jnp.int32) // PMAX
    live = (slot_rank < counts[holder]).astype(jnp.float32)
    cos_part, sin_part = inverse_table()
    scale = 1.0 / math.sqrt(SEGMENTS * NF)

    def one_tile(item):
        pair_ids, alive = item
        left = lax.dynamic_index_in_dim(white, pair_ids[0], axis=1, keepdims=False).astype(jnp.float32)
        right = lax.dynamic_index_in_dim(white, pair_ids[1], axis=1, keepdims=False).astype(jnp.float32)
        left_real, left_imag = (left[..., :NF], left[..., NF:])
        right_real, right_imag = (right[..., :NF], right[..., NF:])
        cross_real = jnp.einsum('sif,sjf->fij', left_real, right_real) + jnp.einsum('sif,sjf->fij', left_imag, right_imag)
        cross_imag = jnp.einsum('sif,sjf->fij', left_real, right_imag) - jnp.einsum('sif,sjf->fij', left_imag, right_real)
        cross_real = cross_real.reshape(NF, BLOCK * BLOCK)
        cross_imag = cross_imag.reshape(NF, BLOCK * BLOCK)
        lagged = jnp.dot(cos_part, cross_real, precision=lax.Precision.HIGHEST)
        lagged = lagged + jnp.dot(sin_part, cross_imag, precision=lax.Precision.HIGHEST)
        return lagged * scale * alive
    return lax.map(one_tile, (stored, live))
```

```python
import functools
import math

import jax
import jax.numpy as jnp
import ml_dtypes
import numpy as np
from jax import lax
from jax.experimental import pallas as pl
from jax.experimental.pallas import tpu as pltpu
from jax.sharding import PartitionSpec as P

BLOCK = 128
NT = 1024
NF = 128
LOW_BIN = 8
LAGS = 128
NG = 16
NZ = 16
NY = 4
NX = 4
NTM = 8
SLOTS = 3
UNITS = 2 * SLOTS
CHUNKS = 4
GC = NG // CHUNKS
BF = jnp.bfloat16
F32 = jnp.float32
MESH = pl.DeviceIdType.MESH


def split(table):
    high = table.astype(np.float32).astype(ml_dtypes.bfloat16)
    low = (table.astype(np.float32) - high.astype(np.float32)).astype(ml_dtypes.bfloat16)
    return high, low


def forward_table():
    samples = np.arange(NT)
    bins = LOW_BIN + np.arange(NF)
    angle = (bins[:, None] * samples[None, :] % NT) * (2.0 * math.pi / NT)
    return split(np.concatenate([np.cos(angle), -np.sin(angle)], axis=0))


def inverse_table():
    shifts = np.arange(LAGS) - LAGS // 2
    bins = LOW_BIN + np.arange(NF)
    angle = (shifts[:, None] * bins[None, :] % NT) * (2.0 * math.pi / NT)
    parts = np.stack([np.cos(angle), -np.sin(angle)], axis=0)
    parts = parts.reshape(2, LAGS, NG, 8).transpose(1, 2, 0, 3)
    return split(parts.reshape(LAGS, 2 * NF))


def nt_dot(a, b):
    return lax.dot_general(a, b, (((1,), (1,)), ((), ())), preferred_element_type=F32)


def exchange_kernel(
    traces, tab_hi, tab_lo, owner, tiles, b_out, p_out,
    slabs, picks, stage_a, stage_d, stage_m, got_x, got_p, got_m,
    packed, choose, req_v, req_s,
    z_send, z_recv, r_send, r_recv, r_loc, a_send, a_recv, d_send, d_recv, m_send, m_recv,
    b_send, b_recv, p_send, p_recv, own_sem,
):
    t = lax.axis_index("tm")
    pair = lax.axis_index("pair")
    z, y = pair // NY, pair % NY
    x, core = t // 2, t % 2

    def at_z(step):
        return {"pair": ((z + step + NZ) % NZ) * NY + y}

    def at_y(step):
        return {"pair": z * NY + (y + step + NY) % NY}

    def at_x(step):
        return {"tm": ((x + step + NX) % NX) * 2 + core}

    def at_t(step):
        return {"tm": (t + step) % NTM}

    sibling = {"tm": x * 2 + 1 - core}

    barrier = pltpu.get_barrier_semaphore()
    greet = [at_z(1), at_z(-1)] + [at_y(d) for d in (1, 2, 3)] + [at_t(d) for d in range(1, NTM)]
    for who in greet:
        pl.semaphore_signal(barrier, inc=1, device_id=who, device_id_type=MESH)

    values = traces[...]
    v_hi = values.astype(BF)
    v_lo = (values - v_hi.astype(F32)).astype(BF)
    spec = nt_dot(tab_hi[...], v_hi) + (nt_dot(tab_hi[...], v_lo) + nt_dot(tab_lo[...], v_hi))
    real, imag = spec[:NF], spec[NF:]
    power = real * real + imag * imag
    width = power.shape[1]
    bin_of = lax.broadcasted_iota(jnp.int32, power.shape, 0)
    total = power
    for step in (1, 2):
        ahead = pltpu.roll(power, NF - step, 0)
        behind = pltpu.roll(power, step, 0)
        total = total + jnp.where(bin_of < NF - step, ahead, 0.0)
        total = total + jnp.where(bin_of >= step, behind, 0.0)
    edge = jnp.minimum(jnp.minimum(bin_of, NF - 1 - bin_of), 2)
    smooth = total / (edge + 3).astype(F32)
    level = jnp.sum(power, axis=0, keepdims=True) * (1.0 / NF)
    factor = lax.rsqrt(smooth + 0.05 * level + 1e-06)
    white = jnp.concatenate(
        [(real * factor).reshape(NG, 8, width), (imag * factor).reshape(NG, 8, width)], axis=1
    ).astype(BF)
    slabs[z, :, 0] = white[:, :, :BLOCK]
    slabs[z, :, 1] = white[:, :, BLOCK:]

    mine = []
    lane = lax.broadcasted_iota(jnp.int32, (8, 128), 1)
    row = jnp.zeros((8, 128), jnp.int32)
    for u in range(UNITS):
        wanted = owner[tiles[u % SLOTS, u // SLOTS]]
        mine.append(wanted)
        row = jnp.where(lane == u, wanted, row)
    req_v[0] = row

    pl.semaphore_wait(barrier, len(greet))

    def z_copy(way, step, c):
        sign = 1 - 2 * way
        index = (z - sign * step + NZ) % NZ
        ref = slabs.at[index, pl.ds(c * GC, GC)]
        return pltpu.make_async_remote_copy(
            src_ref=ref, dst_ref=ref,
            send_sem=z_send.at[way, step, c], recv_sem=z_recv.at[way, step, c],
            device_id=at_z(sign), device_id_type=MESH,
        )

    def z_arrived(way, step, c):
        sign = 1 - 2 * way
        index = (z - sign * (step + 1) + NZ) % NZ
        ref = slabs.at[index, pl.ds(c * GC, GC)]
        pltpu.make_async_remote_copy(
            src_ref=ref, dst_ref=ref,
            send_sem=z_send.at[way, step, c], recv_sem=z_recv.at[way, step, c],
            device_id=at_z(sign), device_id_type=MESH,
        ).wait_recv()

    last = NZ // 2 - 1

    def z_pieces(step):
        for c in range(CHUNKS):
            for way in (0, 1):
                if step < last or (c < CHUNKS // 2) == (way == 0):
                    yield way, c

    z_started = []
    for way, c in z_pieces(0):
        copy = z_copy(way, 0, c)
        copy.start()
        z_started.append(copy)

    r_copies = []
    for d in (1, 2, 3):
        copy = pltpu.make_async_remote_copy(
            src_ref=req_v.at[0], dst_ref=req_v.at[d],
            send_sem=r_send.at[d], recv_sem=r_recv.at[d],
            device_id=at_y(d), device_id_type=MESH,
        )
        copy.start()
        r_copies.append(copy)

    r_i = lax.broadcasted_iota(jnp.int32, (BLOCK, BLOCK), 0)
    c_i = lax.broadcasted_iota(jnp.int32, (BLOCK, BLOCK), 1)
    for to in range(NTM):
        inside = (r_i >= 16 * to) & (r_i < 16 * to + 16)
        for part in range(UNITS):
            hit = inside & (c_i - r_i == 16 * part - 16 * to)
            choose[to, pl.ds(part * BLOCK, BLOCK), :] = jnp.where(hit, 1.0, 0.0).astype(BF)

    for copy in r_copies:
        copy.wait()
    for d in (1, 2, 3):
        local = pltpu.make_async_copy(req_v.at[d], req_s.at[d], r_loc.at[d])
        local.start()
        local.wait()

    for step in range(1, last + 1):
        for way, c in z_pieces(step):
            z_arrived(way, step - 1, c)
            copy = z_copy(way, step, c)
            copy.start()
            z_started.append(copy)
        if step == last:
            for c in range(CHUNKS):
                for way in (0, 1):
                    if (way, c) not in list(z_pieces(last)):
                        z_arrived(way, step - 1, c)
    for way, c in z_pieces(last):
        z_arrived(way, last, c)

    def asked(d, u):
        wanted = mine[u] if d == 0 else req_s[(NY - d) % NY, 0, u]
        return wanted // NY, wanted % NY

    def send(src, dst, s_sem, r_sem, who):
        copy = pltpu.make_async_remote_copy(
            src_ref=src, dst_ref=dst, send_sem=s_sem, recv_sem=r_sem,
            device_id=who, device_id_type=MESH,
        )
        copy.start()
        return copy

    copies = {}

    def first_hop(u):
        index, _ = asked(2, u)
        for s in (0, 1):
            stage_a[u, s] = slabs[index, :, s]
            copies["a", u, s] = send(
                stage_a.at[u, s], got_x.at[u, s], a_send.at[u, s], a_recv.at[u, s],
                at_y(1 if s == 0 else -1),
            )

    def direct(u):
        for s, d, got in ((1, 1, got_p), (0, -1, got_m)):
            index, _ = asked(d % NY, u)
            stage_d[u, s] = slabs[index, :, s]
            copies["d", u, s] = send(
                stage_d.at[u, s], got.at[u, s], d_send.at[u, s], d_recv.at[u, s], at_y(d)
            )

    def merged(u):
        for s, d, got in ((0, 1, got_p), (1, -1, got_m)):
            index, column = asked(d % NY, u)
            copies["a", u, s].wait_recv()
            stage_m[u, s] = jnp.where(column == y, slabs[index, :, s], got_x[u, s])
            copies["m", u, s] = send(
                stage_m.at[u, s], got.at[u, s], m_send.at[u, s], m_recv.at[u, s], at_y(d)
            )

    def finish(u):
        index, column = asked(0, u)
        for s in (0, 1):
            copies["d", u, s].wait_recv()
            copies["m", u, s].wait_recv()
        up, down = (y + 1) % NY, (y + NY - 1) % NY
        own = column == y
        first = jnp.where(column == up, got_m[u, 0], got_p[u, 0])
        picks[u, :, 0] = jnp.where(own, slabs[index, :, 0], first)
        second = jnp.where(column == down, got_p[u, 1], got_m[u, 1])
        picks[u, :, 1] = jnp.where(own, slabs[index, :, 1], second)

    def send_first():
        lanes = jnp.concatenate(
            [picks[u, :, s].reshape(2 * NF, BLOCK) for u in range(SLOTS) for s in (0, 1)], axis=1
        )
        for to in range(NTM):
            packed[to] = jnp.dot(lanes, choose[to], preferred_element_type=F32).astype(BF)
        for d in range(1, NTM):
            to = (t + d) % NTM
            copies["p", d] = send(
                packed.at[to], p_out.at[t], p_send.at[d], p_recv.at[d], at_t(d)
            )
        copies["p", 0] = pltpu.make_async_copy(packed.at[t], p_out.at[t], own_sem.at[SLOTS])
        copies["p", 0].start()

    half = NG // 2

    def t_of(step, c=None):
        return ((x + step + NX) % NX) * 2 + (core if c is None else c)

    def b_send_to(k, n, src, where, who):
        copies["b", k, n] = send(src, where, b_send.at[k, n], b_recv.at[k, n], who)

    def b_arrived(k, n, ref):
        pltpu.make_async_remote_copy(
            src_ref=ref, dst_ref=ref, send_sem=b_send.at[k, n], recv_sem=b_recv.at[k, n],
            device_id=sibling, device_id_type=MESH,
        ).wait_recv()

    def send_second(k):
        mine_ref = picks.at[SLOTS + k]
        b_send_to(k, 0, mine_ref, b_out.at[k, t], at_x(1))
        b_send_to(k, 1, mine_ref, b_out.at[k, t], at_x(-1))
        b_send_to(k, 2, mine_ref, b_out.at[k, t], sibling)
        copies["o", k] = pltpu.make_async_copy(mine_ref, b_out.at[k, t], own_sem.at[k])
        copies["o", k].start()

    lower, upper = pl.ds(0, half), pl.ds(half, half)

    def pass_second(k):
        low = b_out.at[k, t_of(-1)]
        b_arrived(k, 0, low)
        b_send_to(k, 3, b_out.at[k, t_of(-1), lower], b_out.at[k, t_of(-1), lower], at_x(1))
        b_send_to(k, 5, low, low, sibling)
        high = b_out.at[k, t_of(1)]
        b_arrived(k, 1, high)
        b_send_to(k, 4, b_out.at[k, t_of(1), upper], b_out.at[k, t_of(1), upper], at_x(-1))
        b_send_to(k, 6, high, high, sibling)

    def share_second(k):
        far_low = b_out.at[k, t_of(2), lower]
        b_arrived(k, 3, far_low)
        b_send_to(k, 7, far_low, far_low, sibling)
        far_up = b_out.at[k, t_of(2), upper]
        b_arrived(k, 4, far_up)
        b_send_to(k, 8, far_up, far_up, sibling)

    def close_second(k):
        b_arrived(k, 2, b_out.at[k, t_of(0, 1 - core)])
        b_arrived(k, 5, b_out.at[k, t_of(-1, 1 - core)])
        b_arrived(k, 6, b_out.at[k, t_of(1, 1 - core)])
        b_arrived(k, 7, b_out.at[k, t_of(2, 1 - core), lower])
        b_arrived(k, 8, b_out.at[k, t_of(2, 1 - core), upper])

    first_hop(0)
    first_hop(1)
    direct(0)
    for u in range(UNITS + 1):
        if u < UNITS:
            merged(u)
            if u + 2 < UNITS:
                first_hop(u + 2)
            if u + 1 < UNITS:
                direct(u + 1)
        if u >= 1:
            finish(u - 1)
            if u - 1 == SLOTS - 1:
                send_first()
            if u - 1 >= SLOTS:
                send_second(u - 1 - SLOTS)
            if u - 2 >= SLOTS:
                pass_second(u - 2 - SLOTS)
            if u - 3 >= SLOTS:
                share_second(u - 3 - SLOTS)
    pass_second(SLOTS - 1)
    share_second(SLOTS - 2)
    share_second(SLOTS - 1)
    for k in range(SLOTS):
        close_second(k)
        copies["o", k].wait()
    for d in range(1, NTM):
        come = (t + NTM - d) % NTM
        pltpu.make_async_remote_copy(
            src_ref=packed.at[0], dst_ref=p_out.at[come],
            send_sem=p_send.at[d], recv_sem=p_recv.at[d],
            device_id=sibling, device_id_type=MESH,
        ).wait_recv()
    copies["p", 0].wait()
    for copy in z_started:
        copy.wait_send()
    for u in range(UNITS):
        for s in (0, 1):
            for kind in ("a", "d", "m"):
                copies[kind, u, s].wait_send()
    for d in range(1, NTM):
        copies["p", d].wait_send()
    for k in range(SLOTS):
        for n in range(9):
            copies["b", k, n].wait_send()


def exchange(traces, owner, tiles):
    seg_count = traces.shape[0]
    rows = seg_count * BLOCK
    tab_hi, tab_lo = forward_table()
    vmem = pl.BlockSpec(memory_space=pltpu.VMEM)
    smem = pl.BlockSpec(memory_space=pltpu.SMEM)
    anywhere = pl.BlockSpec(memory_space=pl.ANY)
    half_units = (UNITS, 2, NG, 16, BLOCK)
    dma = pltpu.SemaphoreType.DMA
    return pl.pallas_call(
        exchange_kernel,
        out_shape=(
            jax.ShapeDtypeStruct((SLOTS, NTM, NG, 2, 16, BLOCK), BF),
            jax.ShapeDtypeStruct((NTM, 2 * NF, BLOCK), BF),
        ),
        in_specs=[vmem, vmem, vmem, smem, smem],
        out_specs=(anywhere, anywhere),
        scratch_shapes=[
            pltpu.VMEM((NZ, NG, 2, 16, BLOCK), BF),
            pltpu.VMEM((UNITS, NG, 2, 16, BLOCK), BF),
            pltpu.VMEM(half_units, BF),
            pltpu.VMEM(half_units, BF),
            pltpu.VMEM(half_units, BF),
            pltpu.VMEM(half_units, BF),
            pltpu.VMEM(half_units, BF),
            pltpu.VMEM(half_units, BF),
            pltpu.VMEM((NTM, 2 * NF, BLOCK), BF),
            pltpu.VMEM((NTM, UNITS * BLOCK, BLOCK), BF),
            pltpu.VMEM((NY, 8, 128), jnp.int32),
            pltpu.SMEM((NY, 8, 128), jnp.int32),
            dma((2, NZ // 2, CHUNKS)), dma((2, NZ // 2, CHUNKS)),
            dma((NY,)), dma((NY,)), dma((NY,)),
            dma((UNITS, 2)), dma((UNITS, 2)),
            dma((UNITS, 2)), dma((UNITS, 2)),
            dma((UNITS, 2)), dma((UNITS, 2)),
            dma((SLOTS, 9)), dma((SLOTS, 9)),
            dma((NTM,)), dma((NTM,)),
            dma((SLOTS + 1,)),
        ],
        compiler_params=pltpu.CompilerParams(
            collective_id=0, has_side_effects=True, vmem_limit_bytes=48 << 20
        ),
        name="exchange",
    )(traces.reshape(rows, NT), jnp.asarray(tab_hi), jnp.asarray(tab_lo), owner, tiles)


def stack_kernel(scale, counts, p_ref, b_ref, inv_hi, inv_lo, out, first, turned, high, low):
    k = pl.program_id(0)

    @pl.when(k == 0)
    def _():
        eye = (
            lax.broadcasted_iota(jnp.int32, (BLOCK, BLOCK), 0)
            == lax.broadcasted_iota(jnp.int32, (BLOCK, BLOCK), 1)
        )
        eye = jnp.where(eye, 1.0, 0.0).astype(BF)
        for g in range(NG):
            tile = p_ref[:, g * 16 : (g + 1) * 16, :]
            first[g] = nt_dot(eye, tile.reshape(BLOCK, BLOCK))
            wide = tile.astype(F32)
            wide = jnp.concatenate([-wide[:, 8:], wide[:, :8]], axis=1)
            turned[g] = nt_dot(eye, wide.astype(BF).reshape(BLOCK, BLOCK))

    shape = (8, BLOCK)
    mask = lax.broadcasted_iota(jnp.int32, shape, 1) % 8 == lax.broadcasted_iota(
        jnp.int32, shape, 0
    )
    mask = jnp.where(mask, 1.0, 0.0).astype(F32)[None]

    def group(g, carry):
        halves = []
        for s in (0, 1):
            rows = pl.ds(pl.multiple_of(k * 32 + s * 16, 16), 16)
            direct = first[g, rows, :][:, None, :] * mask
            crossed = turned[g, rows, :][:, None, :] * mask
            both = jnp.concatenate([direct, crossed], axis=1).astype(BF)
            halves.append(both.reshape(2 * NF, BLOCK))
        lhs = jnp.concatenate(halves, axis=1)
        rhs = jnp.concatenate([b_ref[t, g, s] for s in (0, 1) for t in range(NTM)], axis=0)
        cross = jnp.dot(lhs, rhs, preferred_element_type=F32).reshape(16, 16, BLOCK)
        rows = pl.ds(pl.multiple_of(g * 16, 16), 16)
        top = cross.astype(BF)
        high[:, rows, :] = top
        low[:, rows, :] = (cross - top.astype(F32)).astype(BF)
        return carry

    lax.fori_loop(0, NG, group, 0)
    factor = jnp.where(k < counts[0], scale, 0.0)
    for i in range(0, 16, 2):
        c_hi = jnp.concatenate([high[i], high[i + 1]], axis=1)
        c_lo = jnp.concatenate([low[i], low[i + 1]], axis=1)
        lagged = jnp.dot(inv_hi[...], c_hi, preferred_element_type=F32)
        lagged = lagged + jnp.dot(inv_lo[...], c_hi, preferred_element_type=F32)
        lagged = lagged + jnp.dot(inv_hi[...], c_lo, preferred_element_type=F32)
        out[:, i * BLOCK : (i + 2) * BLOCK] = lagged * factor


def stack(counts, p_all, b_all, scale):
    inv_hi, inv_lo = inverse_table()
    share = BLOCK // NTM
    return pl.pallas_call(
        functools.partial(stack_kernel, scale),
        grid=(SLOTS,),
        out_shape=jax.ShapeDtypeStruct((SLOTS, LAGS, share * BLOCK), F32),
        in_specs=[
            pl.BlockSpec(memory_space=pltpu.SMEM),
            pl.BlockSpec((NTM, 2 * NF, BLOCK), lambda k: (0, 0, 0)),
            pl.BlockSpec((None, NTM, NG, 2, 16, BLOCK), lambda k: (k, 0, 0, 0, 0, 0)),
            pl.BlockSpec((LAGS, 2 * NF), lambda k: (0, 0)),
            pl.BlockSpec((LAGS, 2 * NF), lambda k: (0, 0)),
        ],
        out_specs=pl.BlockSpec((None, LAGS, share * BLOCK), lambda k: (k, 0, 0)),
        scratch_shapes=[
            pltpu.VMEM((NG, BLOCK, BLOCK), F32),
            pltpu.VMEM((NG, BLOCK, BLOCK), F32),
            pltpu.VMEM((16, 2 * NF, BLOCK), BF),
            pltpu.VMEM((16, 2 * NF, BLOCK), BF),
        ],
        compiler_params=pltpu.CompilerParams(
            dimension_semantics=("arbitrary",), vmem_limit_bytes=32 << 20
        ),
        name="stack",
    )(counts, p_all, b_all, jnp.asarray(inv_hi), jnp.asarray(inv_lo))


def shards(traces, owner, tiles, counts):
    segments = traces.shape[0] * NTM
    b_all, p_all = exchange(traces, owner, tiles)
    return stack(counts, p_all, b_all, 1.0 / math.sqrt(segments * NF))


def solution(mesh):
    placed = (P("tm", "pair", None), P(), P("pair", None), P("pair"))
    return jax.shard_map(
        shards, mesh=mesh, in_specs=placed, out_specs=P("pair", None, "tm"), check_vma=False
    )
```

```python
import functools
import math

import jax
import jax.numpy as jnp
import ml_dtypes
import numpy as np
from jax import lax
from jax.experimental import pallas as pl
from jax.experimental.pallas import tpu as pltpu
from jax.sharding import PartitionSpec as P

BLOCK = 128
NT = 1024
NF = 128
LOW_BIN = 8
LAGS = 128
NG = 16
NZ = 16
NY = 4
NX = 4
NTM = 8
SLOTS = 3
UNITS = 2 * SLOTS
CHUNKS = 4
GC = NG // CHUNKS
BF = jnp.bfloat16
F32 = jnp.float32
MESH = pl.DeviceIdType.MESH


def split(table):
    high = table.astype(np.float32).astype(ml_dtypes.bfloat16)
    low = (table.astype(np.float32) - high.astype(np.float32)).astype(ml_dtypes.bfloat16)
    return high, low


def forward_table():
    samples = np.arange(NT)
    bins = LOW_BIN + np.arange(NF)
    angle = (bins[:, None] * samples[None, :] % NT) * (2.0 * math.pi / NT)
    return split(np.concatenate([np.cos(angle), -np.sin(angle)], axis=0))


def inverse_table():
    shifts = np.arange(LAGS) - LAGS // 2
    bins = LOW_BIN + np.arange(NF)
    angle = (shifts[:, None] * bins[None, :] % NT) * (2.0 * math.pi / NT)
    parts = np.stack([np.cos(angle), -np.sin(angle)], axis=0)
    parts = parts.reshape(2, LAGS, NG, 8).transpose(1, 2, 0, 3)
    return split(parts.reshape(LAGS, 2 * NF))


def in_hbm(array):
    return pltpu.with_memory_space_constraint(jnp.asarray(array), pltpu.HBM)


def nt_dot(a, b):
    return lax.dot_general(a, b, (((1,), (1,)), ((), ())), preferred_element_type=F32)


def exchange_kernel(
    traces_hbm, hi_hbm, lo_hbm, owner_hbm, tiles_hbm, b_out, p_out,
    owner, tiles, traces, tab_hi, tab_lo, load_sem, slabs, picks, stage_a, stage_d, stage_m, got_x, got_p, got_m,
    packed, choose, req_v, req_s,
    z_send, z_recv, r_send, r_recv, r_loc, a_send, a_recv, d_send, d_recv, m_send, m_recv,
    b_send, b_recv, p_send, p_recv, own_sem,
):
    t = lax.axis_index("tm")
    pair = lax.axis_index("pair")
    z, y = pair // NY, pair % NY
    x, core = t // 2, t % 2

    def at_z(step):
        return {"pair": ((z + step + NZ) % NZ) * NY + y}

    def at_y(step):
        return {"pair": z * NY + (y + step + NY) % NY}

    def at_x(step):
        return {"tm": ((x + step + NX) % NX) * 2 + core}

    def at_t(step):
        return {"tm": (t + step) % NTM}

    sibling = {"tm": x * 2 + 1 - core}

    barrier = pltpu.get_barrier_semaphore()
    greet = [at_z(1), at_z(-1)] + [at_y(d) for d in (1, 2, 3)] + [at_t(d) for d in range(1, NTM)]
    for who in greet:
        pl.semaphore_signal(barrier, inc=1, device_id=who, device_id_type=MESH)

    loads = [
        pltpu.make_async_copy(src, dst, load_sem.at[n])
        for n, (src, dst) in enumerate(
            (
                (hi_hbm, tab_hi), (traces_hbm, traces), (lo_hbm, tab_lo),
                (owner_hbm, owner), (tiles_hbm, tiles),
            )
        )
    ]
    for load in loads:
        load.start()
    for load in loads:
        load.wait()

    values = traces[...]
    v_hi = values.astype(BF)
    v_lo = (values - v_hi.astype(F32)).astype(BF)
    spec = nt_dot(tab_hi[...], v_hi) + (nt_dot(tab_hi[...], v_lo) + nt_dot(tab_lo[...], v_hi))
    real, imag = spec[:NF], spec[NF:]
    power = real * real + imag * imag
    width = power.shape[1]
    bin_of = lax.broadcasted_iota(jnp.int32, power.shape, 0)
    total = power
    for step in (1, 2):
        ahead = pltpu.roll(power, NF - step, 0)
        behind = pltpu.roll(power, step, 0)
        total = total + jnp.where(bin_of < NF - step, ahead, 0.0)
        total = total + jnp.where(bin_of >= step, behind, 0.0)
    edge = jnp.minimum(jnp.minimum(bin_of, NF - 1 - bin_of), 2)
    smooth = total / (edge + 3).astype(F32)
    level = jnp.sum(power, axis=0, keepdims=True) * (1.0 / NF)
    factor = lax.rsqrt(smooth + 0.05 * level + 1e-06)
    white = jnp.concatenate(
        [(real * factor).reshape(NG, 8, width), (imag * factor).reshape(NG, 8, width)], axis=1
    ).astype(BF)
    slabs[z, :, 0] = white[:, :, :BLOCK]
    slabs[z, :, 1] = white[:, :, BLOCK:]

    mine = []
    lane = lax.broadcasted_iota(jnp.int32, (8, 128), 1)
    row = jnp.zeros((8, 128), jnp.int32)
    for u in range(UNITS):
        wanted = owner[tiles[u // SLOTS, u % SLOTS]]
        mine.append(wanted)
        row = jnp.where(lane == u, wanted, row)
    req_v[0] = row

    pl.semaphore_wait(barrier, len(greet))

    def z_copy(way, step, c):
        sign = 1 - 2 * way
        index = (z - sign * step + NZ) % NZ
        ref = slabs.at[index, pl.ds(c * GC, GC)]
        return pltpu.make_async_remote_copy(
            src_ref=ref, dst_ref=ref,
            send_sem=z_send.at[way, step, c], recv_sem=z_recv.at[way, step, c],
            device_id=at_z(sign), device_id_type=MESH,
        )

    def z_arrived(way, step, c):
        sign = 1 - 2 * way
        index = (z - sign * (step + 1) + NZ) % NZ
        ref = slabs.at[index, pl.ds(c * GC, GC)]
        pltpu.make_async_remote_copy(
            src_ref=ref, dst_ref=ref,
            send_sem=z_send.at[way, step, c], recv_sem=z_recv.at[way, step, c],
            device_id=at_z(sign), device_id_type=MESH,
        ).wait_recv()

    last = NZ // 2 - 1

    def z_pieces(step):
        for c in range(CHUNKS):
            for way in (0, 1):
                if step < last or (c < CHUNKS // 2) == (way == 0):
                    yield way, c

    z_started = []
    for way, c in z_pieces(0):
        copy = z_copy(way, 0, c)
        copy.start()
        z_started.append(copy)

    r_copies = []
    for d in (1, 2, 3):
        copy = pltpu.make_async_remote_copy(
            src_ref=req_v.at[0], dst_ref=req_v.at[d],
            send_sem=r_send.at[d], recv_sem=r_recv.at[d],
            device_id=at_y(d), device_id_type=MESH,
        )
        copy.start()
        r_copies.append(copy)

    def build_choose(to):
        r_i = lax.broadcasted_iota(jnp.int32, (BLOCK, BLOCK), 0)
        c_i = lax.broadcasted_iota(jnp.int32, (BLOCK, BLOCK), 1)
        inside = (r_i >= 16 * to) & (r_i < 16 * to + 16)
        lanes = slice(to % 2 * BLOCK, to % 2 * BLOCK + BLOCK)
        for part in range(UNITS):
            hit = inside & (c_i - r_i == 16 * part - 16 * to)
            choose[to // 2, pl.ds(part * BLOCK, BLOCK), lanes] = jnp.where(hit, 1.0, 0.0).astype(BF)

    def fetch_requests():
        for copy in r_copies:
            copy.wait()
        local = [
            pltpu.make_async_copy(req_v.at[d], req_s.at[d], r_loc.at[d]) for d in (1, 2, 3)
        ]
        for copy in local:
            copy.start()
        for copy in local:
            copy.wait()

    for step in range(1, last + 1):
        for way, c in z_pieces(step):
            z_arrived(way, step - 1, c)
            copy = z_copy(way, step, c)
            copy.start()
            z_started.append(copy)
        build_choose(step)
        if step == 1:
            build_choose(0)
        if step == 4:
            fetch_requests()
        if step == last:
            for c in range(CHUNKS):
                for way in (0, 1):
                    if (way, c) not in list(z_pieces(last)):
                        z_arrived(way, step - 1, c)
    for way, c in z_pieces(last):
        z_arrived(way, last, c)

    def asked(d, u):
        wanted = mine[u] if d == 0 else req_s[(NY - d) % NY, 0, u]
        return wanted // NY, wanted % NY

    def send(src, dst, s_sem, r_sem, who):
        copy = pltpu.make_async_remote_copy(
            src_ref=src, dst_ref=dst, send_sem=s_sem, recv_sem=r_sem,
            device_id=who, device_id_type=MESH,
        )
        copy.start()
        return copy

    copies = {}

    def first_hop(u):
        index, _ = asked(2, u)
        for s in (0, 1):
            stage_a[u, s] = slabs[index, :, s]
            copies["a", u, s] = send(
                stage_a.at[u, s], got_x.at[u, s], a_send.at[u, s], a_recv.at[u, s],
                at_y(1 if s == 0 else -1),
            )

    def direct(u):
        for s, d, got in ((1, 1, got_p), (0, -1, got_m)):
            index, _ = asked(d % NY, u)
            stage_d[u, s] = slabs[index, :, s]
            copies["d", u, s] = send(
                stage_d.at[u, s], got.at[u, s], d_send.at[u, s], d_recv.at[u, s], at_y(d)
            )

    def merged(u):
        for s, d, got in ((0, 1, got_p), (1, -1, got_m)):
            index, column = asked(d % NY, u)
            copies["a", u, s].wait_recv()
            stage_m[u, s] = jnp.where(column == y, slabs[index, :, s], got_x[u, s])
            copies["m", u, s] = send(
                stage_m.at[u, s], got.at[u, s], m_send.at[u, s], m_recv.at[u, s], at_y(d)
            )

    def finish(u):
        index, column = asked(0, u)
        for s in (0, 1):
            copies["d", u, s].wait_recv()
            copies["m", u, s].wait_recv()
        up, down = (y + 1) % NY, (y + NY - 1) % NY
        own = column == y
        first = jnp.where(column == up, got_m[u, 0], got_p[u, 0])
        picks[u, :, 0] = jnp.where(own, slabs[index, :, 0], first)
        second = jnp.where(column == down, got_p[u, 1], got_m[u, 1])
        picks[u, :, 1] = jnp.where(own, slabs[index, :, 1], second)

    def send_first(pairs):
        lanes = jnp.concatenate(
            [picks[u, :, s].reshape(2 * NF, BLOCK) for u in range(SLOTS) for s in (0, 1)], axis=1
        )
        for two in pairs:
            both = jnp.dot(lanes, choose[two], preferred_element_type=F32).astype(BF)
            packed[2 * two] = both[:, :BLOCK]
            packed[2 * two + 1] = both[:, BLOCK:]

    def start_first():
        for d in range(1, NTM):
            to = (t + d) % NTM
            copies["p", d] = send(
                packed.at[to], p_out.at[t], p_send.at[d], p_recv.at[d], at_t(d)
            )
        copies["p", 0] = pltpu.make_async_copy(packed.at[t], p_out.at[t], own_sem.at[SLOTS])
        copies["p", 0].start()

    half = NG // 2

    def t_of(step, c=None):
        return ((x + step + NX) % NX) * 2 + (core if c is None else c)

    def b_send_to(k, n, src, where, who):
        copies["b", k, n] = send(src, where, b_send.at[k, n], b_recv.at[k, n], who)

    def b_arrived(k, n, ref):
        pltpu.make_async_remote_copy(
            src_ref=ref, dst_ref=ref, send_sem=b_send.at[k, n], recv_sem=b_recv.at[k, n],
            device_id=sibling, device_id_type=MESH,
        ).wait_recv()

    def send_second(k):
        mine_ref = picks.at[SLOTS + k]
        b_send_to(k, 0, mine_ref, b_out.at[k, t], at_x(1))
        b_send_to(k, 1, mine_ref, b_out.at[k, t], at_x(-1))
        b_send_to(k, 2, mine_ref, b_out.at[k, t], sibling)
        copies["o", k] = pltpu.make_async_copy(mine_ref, b_out.at[k, t], own_sem.at[k])
        copies["o", k].start()

    lower, upper = pl.ds(0, half), pl.ds(half, half)

    def pass_second(k):
        low = b_out.at[k, t_of(-1)]
        b_arrived(k, 0, low)
        b_send_to(k, 3, b_out.at[k, t_of(-1), lower], b_out.at[k, t_of(-1), lower], at_x(1))
        b_send_to(k, 5, low, low, sibling)
        high = b_out.at[k, t_of(1)]
        b_arrived(k, 1, high)
        b_send_to(k, 4, b_out.at[k, t_of(1), upper], b_out.at[k, t_of(1), upper], at_x(-1))
        b_send_to(k, 6, high, high, sibling)

    def share_second(k):
        far_low = b_out.at[k, t_of(2), lower]
        b_arrived(k, 3, far_low)
        b_send_to(k, 7, far_low, far_low, sibling)
        far_up = b_out.at[k, t_of(2), upper]
        b_arrived(k, 4, far_up)
        b_send_to(k, 8, far_up, far_up, sibling)

    def close_second(k):
        b_arrived(k, 2, b_out.at[k, t_of(0, 1 - core)])
        b_arrived(k, 5, b_out.at[k, t_of(-1, 1 - core)])
        b_arrived(k, 6, b_out.at[k, t_of(1, 1 - core)])
        b_arrived(k, 7, b_out.at[k, t_of(2, 1 - core), lower])
        b_arrived(k, 8, b_out.at[k, t_of(2, 1 - core), upper])

    first_hop(0)
    first_hop(1)
    direct(0)
    for u in range(UNITS + 1):
        if u < UNITS:
            merged(u)
            if u + 2 < UNITS:
                first_hop(u + 2)
            if u + 1 < UNITS:
                direct(u + 1)
        if u >= 1:
            finish(u - 1)
            if u - 1 == SLOTS - 1:
                send_first((0, 1))
            if u - 1 == SLOTS:
                send_first((2, 3))
                start_first()
            if u - 1 >= SLOTS:
                send_second(u - 1 - SLOTS)
            if u - 2 >= SLOTS:
                pass_second(u - 2 - SLOTS)
            if u - 3 >= SLOTS:
                share_second(u - 3 - SLOTS)
    pass_second(SLOTS - 1)
    share_second(SLOTS - 2)
    share_second(SLOTS - 1)
    for k in range(SLOTS):
        close_second(k)
        copies["o", k].wait()
    for d in range(1, NTM):
        come = (t + NTM - d) % NTM
        pltpu.make_async_remote_copy(
            src_ref=packed.at[0], dst_ref=p_out.at[come],
            send_sem=p_send.at[d], recv_sem=p_recv.at[d],
            device_id=sibling, device_id_type=MESH,
        ).wait_recv()
    copies["p", 0].wait()
    for copy in z_started:
        copy.wait_send()
    for u in range(UNITS):
        for s in (0, 1):
            for kind in ("a", "d", "m"):
                copies[kind, u, s].wait_send()
    for d in range(1, NTM):
        copies["p", d].wait_send()
    for k in range(SLOTS):
        for n in range(9):
            copies["b", k, n].wait_send()


def exchange(traces, owner, tiles):
    seg_count = traces.shape[0]
    rows = seg_count * BLOCK
    tab_hi, tab_lo = forward_table()
    hbm = pl.BlockSpec(memory_space=pltpu.HBM)
    anywhere = pl.BlockSpec(memory_space=pl.ANY)
    half_units = (UNITS, 2, NG, 16, BLOCK)
    dma = pltpu.SemaphoreType.DMA
    return pl.pallas_call(
        exchange_kernel,
        out_shape=(
            jax.ShapeDtypeStruct((SLOTS, NTM, NG, 2, 16, BLOCK), BF),
            jax.ShapeDtypeStruct((NTM, 2 * NF, BLOCK), BF),
        ),
        in_specs=[hbm, hbm, hbm, hbm, hbm],
        out_specs=(anywhere, anywhere),
        scratch_shapes=[
            pltpu.SMEM(owner.shape, jnp.int32),
            pltpu.SMEM(tiles.shape[::-1], jnp.int32),
            pltpu.VMEM((rows, NT), F32),
            pltpu.VMEM((2 * NF, NT), BF),
            pltpu.VMEM((2 * NF, NT), BF),
            dma((5,)),
            pltpu.VMEM((NZ, NG, 2, 16, BLOCK), BF),
            pltpu.VMEM((UNITS, NG, 2, 16, BLOCK), BF),
            pltpu.VMEM(half_units, BF),
            pltpu.VMEM(half_units, BF),
            pltpu.VMEM(half_units, BF),
            pltpu.VMEM(half_units, BF),
            pltpu.VMEM(half_units, BF),
            pltpu.VMEM(half_units, BF),
            pltpu.VMEM((NTM, 2 * NF, BLOCK), BF),
            pltpu.VMEM((NTM // 2, UNITS * BLOCK, 2 * BLOCK), BF),
            pltpu.VMEM((NY, 8, 128), jnp.int32),
            pltpu.SMEM((NY, 8, 128), jnp.int32),
            dma((2, NZ // 2, CHUNKS)), dma((2, NZ // 2, CHUNKS)),
            dma((NY,)), dma((NY,)), dma((NY,)),
            dma((UNITS, 2)), dma((UNITS, 2)),
            dma((UNITS, 2)), dma((UNITS, 2)),
            dma((UNITS, 2)), dma((UNITS, 2)),
            dma((SLOTS, 9)), dma((SLOTS, 9)),
            dma((NTM,)), dma((NTM,)),
            dma((SLOTS + 1,)),
        ],
        compiler_params=pltpu.CompilerParams(
            collective_id=0, has_side_effects=True, vmem_limit_bytes=48 << 20
        ),
        name="exchange",
    )(*[in_hbm(a) for a in (traces.reshape(rows, NT), tab_hi, tab_lo, owner, tiles.T)])


def stack_kernel(scale, counts, p_ref, b_ref, inv_hi, inv_lo, out, first, turned, high, low):
    k = pl.program_id(0)

    @pl.when(k == 0)
    def _():
        eye = (
            lax.broadcasted_iota(jnp.int32, (BLOCK, BLOCK), 0)
            == lax.broadcasted_iota(jnp.int32, (BLOCK, BLOCK), 1)
        )
        eye = jnp.where(eye, 1.0, 0.0).astype(BF)
        for g in range(NG):
            tile = p_ref[:, g * 16 : (g + 1) * 16, :]
            first[g] = nt_dot(eye, tile.reshape(BLOCK, BLOCK))
            wide = tile.astype(F32)
            wide = jnp.concatenate([-wide[:, 8:], wide[:, :8]], axis=1)
            turned[g] = nt_dot(eye, wide.astype(BF).reshape(BLOCK, BLOCK))

    shape = (8, BLOCK)
    mask = lax.broadcasted_iota(jnp.int32, shape, 1) % 8 == lax.broadcasted_iota(
        jnp.int32, shape, 0
    )
    mask = jnp.where(mask, 1.0, 0.0).astype(F32)[None]

    def group(g):
        halves = []
        for s in (0, 1):
            rows = pl.ds(pl.multiple_of(k * 32 + s * 16, 16), 16)
            direct = first[g, rows, :][:, None, :] * mask
            crossed = turned[g, rows, :][:, None, :] * mask
            both = jnp.concatenate([direct, crossed], axis=1).astype(BF)
            halves.append(both.reshape(2 * NF, BLOCK))
        lhs = jnp.concatenate(halves, axis=1)
        rhs = jnp.concatenate([b_ref[t, g, s] for s in (0, 1) for t in range(NTM)], axis=0)
        cross = jnp.dot(lhs, rhs, preferred_element_type=F32).reshape(16, 16, BLOCK)
        rows = slice(g * 16, g * 16 + 16)
        top = cross.astype(BF)
        high[:, rows, :] = top
        low[:, rows, :] = (cross - top.astype(F32)).astype(BF)

    for g in range(NG):
        group(g)
    factor = jnp.where(k < counts[0], scale, 0.0)
    for i in range(0, 16, 2):
        c_hi = jnp.concatenate([high[i], high[i + 1]], axis=1)
        c_lo = jnp.concatenate([low[i], low[i + 1]], axis=1)
        lagged = jnp.dot(inv_hi[...], c_hi, preferred_element_type=F32)
        lagged = lagged + jnp.dot(inv_lo[...], c_hi, preferred_element_type=F32)
        lagged = lagged + jnp.dot(inv_hi[...], c_lo, preferred_element_type=F32)
        out[:, i * BLOCK : (i + 2) * BLOCK] = lagged * factor


def stack(counts, p_all, b_all, scale):
    inv_hi, inv_lo = inverse_table()
    share = BLOCK // NTM
    return pl.pallas_call(
        functools.partial(stack_kernel, scale),
        grid=(SLOTS,),
        out_shape=jax.ShapeDtypeStruct((SLOTS, LAGS, share * BLOCK), F32),
        in_specs=[
            pl.BlockSpec(memory_space=pltpu.SMEM),
            pl.BlockSpec((NTM, 2 * NF, BLOCK), lambda k: (0, 0, 0)),
            pl.BlockSpec((None, NTM, NG, 2, 16, BLOCK), lambda k: (k, 0, 0, 0, 0, 0)),
            pl.BlockSpec((LAGS, 2 * NF), lambda k: (0, 0)),
            pl.BlockSpec((LAGS, 2 * NF), lambda k: (0, 0)),
        ],
        out_specs=pl.BlockSpec((None, LAGS, share * BLOCK), lambda k: (k, 0, 0)),
        scratch_shapes=[
            pltpu.VMEM((NG, BLOCK, BLOCK), F32),
            pltpu.VMEM((NG, BLOCK, BLOCK), F32),
            pltpu.VMEM((16, 2 * NF, BLOCK), BF),
            pltpu.VMEM((16, 2 * NF, BLOCK), BF),
        ],
        compiler_params=pltpu.CompilerParams(
            dimension_semantics=("arbitrary",), vmem_limit_bytes=32 << 20
        ),
        name="stack",
    )(counts, p_all, b_all, in_hbm(inv_hi), in_hbm(inv_lo))


def shards(traces, owner, tiles, counts):
    segments = traces.shape[0] * NTM
    b_all, p_all = exchange(traces, owner, tiles)
    return stack(counts, p_all, b_all, 1.0 / math.sqrt(segments * NF))


def solution(mesh):
    placed = (P("tm", "pair", None), P(), P("pair", None), P("pair"))
    return jax.shard_map(
        shards, mesh=mesh, in_specs=placed, out_specs=P("pair", None, "tm"), check_vma=False
    )
```

```python
import functools
import math

import jax
import jax.numpy as jnp
import ml_dtypes
import numpy as np
from jax import lax
from jax.experimental import pallas as pl
from jax.experimental.pallas import tpu as pltpu
from jax.sharding import PartitionSpec as P

BLOCK = 128
NT = 1024
NF = 128
LOW_BIN = 8
LAGS = 128
NG = 16
NZ = 16
NY = 4
NX = 4
NTM = 8
SLOTS = 3
UNITS = 2 * SLOTS
CHUNKS = 4
GC = NG // CHUNKS
BF = jnp.bfloat16
F32 = jnp.float32
MESH = pl.DeviceIdType.MESH


def split(table):
    high = table.astype(np.float32).astype(ml_dtypes.bfloat16)
    low = (table.astype(np.float32) - high.astype(np.float32)).astype(ml_dtypes.bfloat16)
    return high, low


def forward_table():
    samples = np.arange(NT)
    bins = LOW_BIN + np.arange(NF)
    angle = (bins[:, None] * samples[None, :] % NT) * (2.0 * math.pi / NT)
    return split(np.concatenate([np.cos(angle), -np.sin(angle)], axis=0))


def inverse_table():
    shifts = np.arange(LAGS) - LAGS // 2
    bins = LOW_BIN + np.arange(NF)
    angle = (shifts[:, None] * bins[None, :] % NT) * (2.0 * math.pi / NT)
    parts = np.stack([np.cos(angle), -np.sin(angle)], axis=0)
    parts = parts.reshape(2, LAGS, NG, 8).transpose(1, 2, 0, 3)
    return split(parts.reshape(LAGS, 2 * NF))


def in_hbm(array):
    return pltpu.with_memory_space_constraint(jnp.asarray(array), pltpu.HBM)


def nt_dot(a, b):
    return lax.dot_general(a, b, (((1,), (1,)), ((), ())), preferred_element_type=F32)


def identity(size):
    row = lax.broadcasted_iota(jnp.int32, (size, size), 0)
    return jnp.where(row == lax.broadcasted_iota(jnp.int32, (size, size), 1), 1.0, 0.0).astype(BF)


def exchange_kernel(
    traces_hbm, hi_hbm, lo_hbm, owner_hbm, tiles_hbm, b_out, p_out,
    owner, tiles, traces, tab_hi, tab_lo, load_sem, slabs, picks, stage_a, stage_d, stage_m, got_x, got_p, got_m,
    packed, req_v, req_s,
    z_send, z_recv, r_send, r_recv, r_loc, a_send, a_recv, d_send, d_recv, m_send, m_recv,
    b_send, b_recv, p_send, p_recv, own_sem,
):
    t = lax.axis_index("tm")
    pair = lax.axis_index("pair")
    z, y = pair // NY, pair % NY
    x, core = t // 2, t % 2

    def at_z(step):
        return {"pair": ((z + step + NZ) % NZ) * NY + y}

    def at_y(step):
        return {"pair": z * NY + (y + step + NY) % NY}

    def at_x(step):
        return {"tm": ((x + step + NX) % NX) * 2 + core}

    def at_t(step):
        return {"tm": (t + step) % NTM}

    sibling = {"tm": x * 2 + 1 - core}

    barrier = pltpu.get_barrier_semaphore()
    greet = [at_z(1), at_z(-1)] + [at_y(d) for d in (1, 2, 3)] + [at_t(d) for d in range(1, NTM)]
    for who in greet:
        pl.semaphore_signal(barrier, inc=1, device_id=who, device_id_type=MESH)

    loads = [
        pltpu.make_async_copy(src, dst, load_sem.at[n])
        for n, (src, dst) in enumerate(
            (
                (hi_hbm, tab_hi), (traces_hbm, traces), (lo_hbm, tab_lo),
                (owner_hbm, owner), (tiles_hbm, tiles),
            )
        )
    ]
    for load in loads:
        load.start()
    for load in loads:
        load.wait()

    values = traces[...]
    v_hi = values.astype(BF)
    v_lo = (values - v_hi.astype(F32)).astype(BF)
    spec = nt_dot(tab_hi[...], v_hi) + (nt_dot(tab_hi[...], v_lo) + nt_dot(tab_lo[...], v_hi))
    real, imag = spec[:NF], spec[NF:]
    power = real * real + imag * imag
    width = power.shape[1]
    bin_of = lax.broadcasted_iota(jnp.int32, power.shape, 0)
    total = power
    for step in (1, 2):
        ahead = pltpu.roll(power, NF - step, 0)
        behind = pltpu.roll(power, step, 0)
        total = total + jnp.where(bin_of < NF - step, ahead, 0.0)
        total = total + jnp.where(bin_of >= step, behind, 0.0)
    edge = jnp.minimum(jnp.minimum(bin_of, NF - 1 - bin_of), 2)
    smooth = total / (edge + 3).astype(F32)
    level = jnp.sum(power, axis=0, keepdims=True) * (1.0 / NF)
    factor = lax.rsqrt(smooth + 0.05 * level + 1e-06)
    white = jnp.concatenate(
        [(real * factor).reshape(NG, 8, width), (imag * factor).reshape(NG, 8, width)], axis=1
    ).astype(BF)
    slabs[z, :, 0] = white[:, :, :BLOCK]
    slabs[z, :, 1] = white[:, :, BLOCK:]

    mine = []
    lane = lax.broadcasted_iota(jnp.int32, (8, 128), 1)
    row = jnp.zeros((8, 128), jnp.int32)
    for u in range(UNITS):
        wanted = owner[tiles[1 - u % 2, u // 2]]
        mine.append(wanted)
        row = jnp.where(lane == u, wanted, row)
    req_v[0] = row

    pl.semaphore_wait(barrier, len(greet))

    def z_copy(way, step, c):
        sign = 1 - 2 * way
        index = (z - sign * step + NZ) % NZ
        ref = slabs.at[index, pl.ds(c * GC, GC)]
        return pltpu.make_async_remote_copy(
            src_ref=ref, dst_ref=ref,
            send_sem=z_send.at[way, step, c], recv_sem=z_recv.at[way, step, c],
            device_id=at_z(sign), device_id_type=MESH,
        )

    def z_arrived(way, step, c):
        sign = 1 - 2 * way
        index = (z - sign * (step + 1) + NZ) % NZ
        ref = slabs.at[index, pl.ds(c * GC, GC)]
        pltpu.make_async_remote_copy(
            src_ref=ref, dst_ref=ref,
            send_sem=z_send.at[way, step, c], recv_sem=z_recv.at[way, step, c],
            device_id=at_z(sign), device_id_type=MESH,
        ).wait_recv()

    last = NZ // 2 - 1

    def z_pieces(step):
        for c in range(CHUNKS):
            for way in (0, 1):
                if step < last or (c < CHUNKS // 2) == (way == 0):
                    yield way, c

    z_started = []
    for way, c in z_pieces(0):
        copy = z_copy(way, 0, c)
        copy.start()
        z_started.append(copy)

    r_copies = []
    for d in (1, 2, 3):
        copy = pltpu.make_async_remote_copy(
            src_ref=req_v.at[0], dst_ref=req_v.at[d],
            send_sem=r_send.at[d], recv_sem=r_recv.at[d],
            device_id=at_y(d), device_id_type=MESH,
        )
        copy.start()
        r_copies.append(copy)

    def fetch_requests():
        for copy in r_copies:
            copy.wait()
        local = [
            pltpu.make_async_copy(req_v.at[d], req_s.at[d], r_loc.at[d]) for d in (1, 2, 3)
        ]
        for copy in local:
            copy.start()
        for copy in local:
            copy.wait()

    for step in range(1, last + 1):
        for way, c in z_pieces(step):
            z_arrived(way, step - 1, c)
            copy = z_copy(way, step, c)
            copy.start()
            z_started.append(copy)
        if step == 4:
            fetch_requests()
        if step == last:
            for c in range(CHUNKS):
                for way in (0, 1):
                    if (way, c) not in list(z_pieces(last)):
                        z_arrived(way, step - 1, c)
    for way, c in z_pieces(last):
        z_arrived(way, last, c)

    def asked(d, u):
        wanted = mine[u] if d == 0 else req_s[(NY - d) % NY, 0, u]
        return wanted // NY, wanted % NY

    def send(src, dst, s_sem, r_sem, who):
        copy = pltpu.make_async_remote_copy(
            src_ref=src, dst_ref=dst, send_sem=s_sem, recv_sem=r_sem,
            device_id=who, device_id_type=MESH,
        )
        copy.start()
        return copy

    copies = {}
    eye = identity(BLOCK)

    def first_hop(u):
        index, _ = asked(2, u)
        for s in (0, 1):
            stage_a[u, s] = slabs[index, :, s]
            copies["a", u, s] = send(
                stage_a.at[u, s], got_x.at[u, s], a_send.at[u, s], a_recv.at[u, s],
                at_y(1 if s == 0 else -1),
            )

    def direct(u):
        for s, d, got in ((1, 1, got_p), (0, -1, got_m)):
            index, _ = asked(d % NY, u)
            stage_d[u, s] = slabs[index, :, s]
            copies["d", u, s] = send(
                stage_d.at[u, s], got.at[u, s], d_send.at[u, s], d_recv.at[u, s], at_y(d)
            )

    def merged(u):
        for s, d, got in ((0, 1, got_p), (1, -1, got_m)):
            index, column = asked(d % NY, u)
            copies["a", u, s].wait_recv()
            stage_m[u, s] = jnp.where(column == y, slabs[index, :, s], got_x[u, s])
            copies["m", u, s] = send(
                stage_m.at[u, s], got.at[u, s], m_send.at[u, s], m_recv.at[u, s], at_y(d)
            )

    def finish(u):
        index, column = asked(0, u)
        for s in (0, 1):
            copies["d", u, s].wait_recv()
            copies["m", u, s].wait_recv()
        up, down = (y + 1) % NY, (y + NY - 1) % NY
        own = column == y
        low = jnp.where(column == up, got_m[u, 0], got_p[u, 0])
        low = jnp.where(own, slabs[index, :, 0], low)
        high = jnp.where(column == down, got_p[u, 1], got_m[u, 1])
        high = jnp.where(own, slabs[index, :, 1], high)
        return low, high

    def send_first(k, value):
        for seg in (0, 1):
            turned = nt_dot(eye, value[seg].reshape(2 * NF, BLOCK)).astype(BF)
            packed[k, :, seg] = turned.reshape(NTM, 16, 2 * NF)
        for d in range(1, NTM):
            to = (t + d) % NTM
            copies["p", k, d] = send(
                packed.at[k, to], p_out.at[t, k], p_send.at[k, d], p_recv.at[k, d], at_t(d)
            )
        copies["p", k, 0] = pltpu.make_async_copy(
            packed.at[k, t], p_out.at[t, k], own_sem.at[SLOTS + k]
        )
        copies["p", k, 0].start()

    half = NG // 2

    def t_of(step, c=None):
        return ((x + step + NX) % NX) * 2 + (core if c is None else c)

    def b_send_to(k, n, src, where, who):
        copies["b", k, n] = send(src, where, b_send.at[k, n], b_recv.at[k, n], who)

    def b_arrived(k, n, ref):
        pltpu.make_async_remote_copy(
            src_ref=ref, dst_ref=ref, send_sem=b_send.at[k, n], recv_sem=b_recv.at[k, n],
            device_id=sibling, device_id_type=MESH,
        ).wait_recv()

    def send_second(k, value):
        picks[k, :, 0], picks[k, :, 1] = value
        mine_ref = picks.at[k]
        b_send_to(k, 0, mine_ref, b_out.at[k, t], at_x(1))
        b_send_to(k, 1, mine_ref, b_out.at[k, t], at_x(-1))
        b_send_to(k, 2, mine_ref, b_out.at[k, t], sibling)
        copies["o", k] = pltpu.make_async_copy(mine_ref, b_out.at[k, t], own_sem.at[k])
        copies["o", k].start()

    lower, upper = pl.ds(0, half), pl.ds(half, half)

    def pass_second(k):
        low = b_out.at[k, t_of(-1)]
        b_arrived(k, 0, low)
        b_send_to(k, 3, b_out.at[k, t_of(-1), lower], b_out.at[k, t_of(-1), lower], at_x(1))
        b_send_to(k, 5, low, low, sibling)
        high = b_out.at[k, t_of(1)]
        b_arrived(k, 1, high)
        b_send_to(k, 4, b_out.at[k, t_of(1), upper], b_out.at[k, t_of(1), upper], at_x(-1))
        b_send_to(k, 6, high, high, sibling)

    def share_second(k):
        far_low = b_out.at[k, t_of(2), lower]
        b_arrived(k, 3, far_low)
        b_send_to(k, 7, far_low, far_low, sibling)
        far_up = b_out.at[k, t_of(2), upper]
        b_arrived(k, 4, far_up)
        b_send_to(k, 8, far_up, far_up, sibling)

    def close_second(k):
        b_arrived(k, 2, b_out.at[k, t_of(0, 1 - core)])
        b_arrived(k, 5, b_out.at[k, t_of(-1, 1 - core)])
        b_arrived(k, 6, b_out.at[k, t_of(1, 1 - core)])
        b_arrived(k, 7, b_out.at[k, t_of(2, 1 - core), lower])
        b_arrived(k, 8, b_out.at[k, t_of(2, 1 - core), upper])

    first_hop(0)
    first_hop(1)
    direct(0)
    for u in range(UNITS + 1):
        if u < UNITS:
            merged(u)
            if u + 2 < UNITS:
                first_hop(u + 2)
            if u + 1 < UNITS:
                direct(u + 1)
        if u == 0:
            continue
        k, role = (u - 1) // 2, (u - 1) % 2
        value = finish(u - 1)
        if role == 0:
            send_second(k, value)
            if k > 0:
                share_second(k - 1)
        else:
            send_first(k, value)
            pass_second(k)
    share_second(SLOTS - 1)
    for k in range(SLOTS):
        close_second(k)
        copies["o", k].wait()
    for k in range(SLOTS):
        for d in range(1, NTM):
            come = (t + NTM - d) % NTM
            pltpu.make_async_remote_copy(
                src_ref=packed.at[k, 0], dst_ref=p_out.at[come, k],
                send_sem=p_send.at[k, d], recv_sem=p_recv.at[k, d],
                device_id=sibling, device_id_type=MESH,
            ).wait_recv()
        copies["p", k, 0].wait()
    for copy in z_started:
        copy.wait_send()
    for u in range(UNITS):
        for s in (0, 1):
            for kind in ("a", "d", "m"):
                copies[kind, u, s].wait_send()
    for k in range(SLOTS):
        for d in range(1, NTM):
            copies["p", k, d].wait_send()
        for n in range(9):
            copies["b", k, n].wait_send()


def exchange(traces, owner, tiles):
    seg_count = traces.shape[0]
    rows = seg_count * BLOCK
    tab_hi, tab_lo = forward_table()
    hbm = pl.BlockSpec(memory_space=pltpu.HBM)
    anywhere = pl.BlockSpec(memory_space=pl.ANY)
    half_units = (UNITS, 2, NG, 16, BLOCK)
    dma = pltpu.SemaphoreType.DMA
    return pl.pallas_call(
        exchange_kernel,
        out_shape=(
            jax.ShapeDtypeStruct((SLOTS, NTM, NG, 2, 16, BLOCK), BF),
            jax.ShapeDtypeStruct((NTM, SLOTS, 2, 16, 2 * NF), BF),
        ),
        in_specs=[hbm, hbm, hbm, hbm, hbm],
        out_specs=(anywhere, anywhere),
        scratch_shapes=[
            pltpu.SMEM(owner.shape, jnp.int32),
            pltpu.SMEM(tiles.shape[::-1], jnp.int32),
            pltpu.VMEM((rows, NT), F32),
            pltpu.VMEM((2 * NF, NT), BF),
            pltpu.VMEM((2 * NF, NT), BF),
            dma((5,)),
            pltpu.VMEM((NZ, NG, 2, 16, BLOCK), BF),
            pltpu.VMEM((SLOTS, NG, 2, 16, BLOCK), BF),
            pltpu.VMEM(half_units, BF),
            pltpu.VMEM(half_units, BF),
            pltpu.VMEM(half_units, BF),
            pltpu.VMEM(half_units, BF),
            pltpu.VMEM(half_units, BF),
            pltpu.VMEM(half_units, BF),
            pltpu.VMEM((SLOTS, NTM, 2, 16, 2 * NF), BF),
            pltpu.VMEM((NY, 8, 128), jnp.int32),
            pltpu.SMEM((NY, 8, 128), jnp.int32),
            dma((2, NZ // 2, CHUNKS)), dma((2, NZ // 2, CHUNKS)),
            dma((NY,)), dma((NY,)), dma((NY,)),
            dma((UNITS, 2)), dma((UNITS, 2)),
            dma((UNITS, 2)), dma((UNITS, 2)),
            dma((UNITS, 2)), dma((UNITS, 2)),
            dma((SLOTS, 9)), dma((SLOTS, 9)),
            dma((SLOTS, NTM)), dma((SLOTS, NTM)),
            dma((2 * SLOTS,)),
        ],
        compiler_params=pltpu.CompilerParams(
            collective_id=0, has_side_effects=True, vmem_limit_bytes=48 << 20
        ),
        name="exchange",
    )(*[in_hbm(a) for a in (traces.reshape(rows, NT), tab_hi, tab_lo, owner, tiles.T)])


def stack_kernel(scale, counts, p_ref, b_ref, inv_hi, inv_lo, out, natural, first, turned, high, low):
    k = pl.program_id(0)

    @pl.when(k == 0)
    def _():
        eye = identity(2 * NF)
        used = SLOTS * 32
        pad = jnp.zeros((2 * NF, BLOCK - used), BF)
        for t in range(NTM):
            back = nt_dot(eye, p_ref[t].reshape(used, 2 * NF)).astype(BF)
            natural[t] = jnp.concatenate([back, pad], axis=1)
        eye = identity(BLOCK)
        for g in range(NG):
            tile = natural[:, g * 16 : (g + 1) * 16, :]
            first[g] = nt_dot(eye, tile.reshape(BLOCK, BLOCK))
            wide = tile.astype(F32)
            wide = jnp.concatenate([-wide[:, 8:], wide[:, :8]], axis=1)
            turned[g] = nt_dot(eye, wide.astype(BF).reshape(BLOCK, BLOCK))

    shape = (8, BLOCK)
    mask = lax.broadcasted_iota(jnp.int32, shape, 1) % 8 == lax.broadcasted_iota(
        jnp.int32, shape, 0
    )
    mask = jnp.where(mask, 1.0, 0.0).astype(F32)[None]

    def group(g):
        halves = []
        for s in (0, 1):
            rows = pl.ds(pl.multiple_of(k * 32 + s * 16, 16), 16)
            direct = first[g, rows, :][:, None, :] * mask
            crossed = turned[g, rows, :][:, None, :] * mask
            both = jnp.concatenate([direct, crossed], axis=1).astype(BF)
            halves.append(both.reshape(2 * NF, BLOCK))
        lhs = jnp.concatenate(halves, axis=1)
        rhs = jnp.concatenate([b_ref[t, g, s] for s in (0, 1) for t in range(NTM)], axis=0)
        cross = jnp.dot(lhs, rhs, preferred_element_type=F32).reshape(16, 16, BLOCK)
        rows = slice(g * 16, g * 16 + 16)
        top = cross.astype(BF)
        high[:, rows, :] = top
        low[:, rows, :] = (cross - top.astype(F32)).astype(BF)

    for g in range(NG):
        group(g)
    factor = jnp.where(k < counts[0], scale, 0.0)
    for i in range(0, 16, 2):
        c_hi = jnp.concatenate([high[i], high[i + 1]], axis=1)
        c_lo = jnp.concatenate([low[i], low[i + 1]], axis=1)
        lagged = jnp.dot(inv_hi[...], c_hi, preferred_element_type=F32)
        lagged = lagged + jnp.dot(inv_lo[...], c_hi, preferred_element_type=F32)
        lagged = lagged + jnp.dot(inv_hi[...], c_lo, preferred_element_type=F32)
        out[:, i * BLOCK : (i + 2) * BLOCK] = lagged * factor


def stack(counts, p_all, b_all, scale):
    inv_hi, inv_lo = inverse_table()
    share = BLOCK // NTM
    return pl.pallas_call(
        functools.partial(stack_kernel, scale),
        grid=(SLOTS,),
        out_shape=jax.ShapeDtypeStruct((SLOTS, LAGS, share * BLOCK), F32),
        in_specs=[
            pl.BlockSpec(memory_space=pltpu.SMEM),
            pl.BlockSpec((NTM, SLOTS, 2, 16, 2 * NF), lambda k: (0, 0, 0, 0, 0)),
            pl.BlockSpec((None, NTM, NG, 2, 16, BLOCK), lambda k: (k, 0, 0, 0, 0, 0)),
            pl.BlockSpec((LAGS, 2 * NF), lambda k: (0, 0)),
            pl.BlockSpec((LAGS, 2 * NF), lambda k: (0, 0)),
        ],
        out_specs=pl.BlockSpec((None, LAGS, share * BLOCK), lambda k: (k, 0, 0)),
        scratch_shapes=[
            pltpu.VMEM((NTM, 2 * NF, BLOCK), BF),
            pltpu.VMEM((NG, BLOCK, BLOCK), F32),
            pltpu.VMEM((NG, BLOCK, BLOCK), F32),
            pltpu.VMEM((16, 2 * NF, BLOCK), BF),
            pltpu.VMEM((16, 2 * NF, BLOCK), BF),
        ],
        compiler_params=pltpu.CompilerParams(
            dimension_semantics=("arbitrary",), vmem_limit_bytes=32 << 20
        ),
        name="stack",
    )(counts, p_all, b_all, in_hbm(inv_hi), in_hbm(inv_lo))


def shards(traces, owner, tiles, counts):
    segments = traces.shape[0] * NTM
    b_all, p_all = exchange(traces, owner, tiles)
    return stack(counts, p_all, b_all, 1.0 / math.sqrt(segments * NF))


def solution(mesh):
    placed = (P("tm", "pair", None), P(), P("pair", None), P("pair"))
    return jax.shard_map(
        shards, mesh=mesh, in_specs=placed, out_specs=P("pair", None, "tm"), check_vma=False
    )
```

```python
import functools
import math

import jax
import jax.numpy as jnp
import ml_dtypes
import numpy as np
from jax import lax
from jax.experimental import pallas as pl
from jax.experimental.pallas import tpu as pltpu
from jax.sharding import PartitionSpec as P

BLOCK = 128
NT = 1024
NF = 128
LOW_BIN = 8
LAGS = 128
NG = 16
NZ = 16
NY = 4
NX = 4
NTM = 8
SLOTS = 3
UNITS = 2 * SLOTS
CHUNKS = 4
GC = 2 * NG // CHUNKS
BF = jnp.bfloat16
F32 = jnp.float32
MESH = pl.DeviceIdType.MESH


def split(table):
    high = table.astype(np.float32).astype(ml_dtypes.bfloat16)
    low = (table.astype(np.float32) - high.astype(np.float32)).astype(ml_dtypes.bfloat16)
    return high, low


def forward_table():
    samples = np.arange(NT)
    bins = LOW_BIN + np.arange(NF)
    angle = (bins[:, None] * samples[None, :] % NT) * (2.0 * math.pi / NT)
    return split(np.concatenate([np.cos(angle), -np.sin(angle)], axis=0))


def inverse_table():
    shifts = np.arange(LAGS) - LAGS // 2
    bins = LOW_BIN + np.arange(NF)
    angle = (shifts[:, None] * bins[None, :] % NT) * (2.0 * math.pi / NT)
    parts = np.stack([np.cos(angle), -np.sin(angle)], axis=0)
    parts = parts.reshape(2, LAGS, NG, 8).transpose(1, 2, 0, 3)
    return split(parts.reshape(LAGS, 2 * NF))


def in_hbm(array):
    return pltpu.with_memory_space_constraint(jnp.asarray(array), pltpu.HBM)


def nt_dot(a, b):
    return lax.dot_general(a, b, (((1,), (1,)), ((), ())), preferred_element_type=F32)


def identity(size):
    row = lax.broadcasted_iota(jnp.int32, (size, size), 0)
    return jnp.where(row == lax.broadcasted_iota(jnp.int32, (size, size), 1), 1.0, 0.0).astype(BF)


def exchange_kernel(
    traces_hbm, hi_hbm, lo_hbm, owner_hbm, tiles_hbm, b_out, p_out,
    owner, tiles, traces, tab_hi, tab_lo, load_sem, slabs, picks, stage_a, stage_d, stage_m, got_x, got_p, got_m,
    packed, req_v, req_s,
    z_send, z_recv, r_send, r_recv, r_loc, a_send, a_recv, d_send, d_recv, m_send, m_recv,
    b_send, b_recv, p_send, p_recv, own_sem,
):
    t = lax.axis_index("tm")
    pair = lax.axis_index("pair")
    z, y = pair // NY, pair % NY
    x, core = t // 2, t % 2

    def at_z(step):
        return {"pair": ((z + step + NZ) % NZ) * NY + y}

    def at_y(step):
        return {"pair": z * NY + (y + step + NY) % NY}

    def at_x(step):
        return {"tm": ((x + step + NX) % NX) * 2 + core}

    def at_t(step):
        return {"tm": (t + step) % NTM}

    sibling = {"tm": x * 2 + 1 - core}

    barrier = pltpu.get_barrier_semaphore()
    greet = [at_z(1), at_z(-1)] + [at_y(d) for d in (1, 2, 3)] + [at_t(d) for d in range(1, NTM)]
    for who in greet:
        pl.semaphore_signal(barrier, inc=1, device_id=who, device_id_type=MESH)

    def load(n, src, dst):
        copy = pltpu.make_async_copy(src, dst, load_sem.at[n])
        copy.start()
        return copy

    rows = [pl.ds(seg * BLOCK, BLOCK) for seg in (0, 1)]
    early = [
        load(0, owner_hbm, owner), load(1, tiles_hbm, tiles),
        load(2, traces_hbm.at[rows[0]], traces.at[rows[0]]),
        load(3, hi_hbm, tab_hi), load(4, lo_hbm, tab_lo),
    ]
    late = load(5, traces_hbm.at[rows[1]], traces.at[rows[1]])
    for copy in early:
        copy.wait()

    def transform(seg):
        values = traces[rows[seg], :]
        v_hi = values.astype(BF)
        v_lo = (values - v_hi.astype(F32)).astype(BF)
        spec = nt_dot(tab_hi[...], v_hi) + (nt_dot(tab_hi[...], v_lo) + nt_dot(tab_lo[...], v_hi))
        real, imag = spec[:NF], spec[NF:]
        power = real * real + imag * imag
        bin_of = lax.broadcasted_iota(jnp.int32, power.shape, 0)
        total = power
        for step in (1, 2):
            ahead = pltpu.roll(power, NF - step, 0)
            behind = pltpu.roll(power, step, 0)
            total = total + jnp.where(bin_of < NF - step, ahead, 0.0)
            total = total + jnp.where(bin_of >= step, behind, 0.0)
        edge = jnp.minimum(jnp.minimum(bin_of, NF - 1 - bin_of), 2)
        smooth = total / (edge + 3).astype(F32)
        level = jnp.sum(power, axis=0, keepdims=True) * (1.0 / NF)
        factor = lax.rsqrt(smooth + 0.05 * level + 1e-06)
        slabs[z, seg] = jnp.concatenate(
            [(real * factor).reshape(NG, 8, BLOCK), (imag * factor).reshape(NG, 8, BLOCK)], axis=1
        ).astype(BF)

    transform(0)

    mine = []
    lane = lax.broadcasted_iota(jnp.int32, (8, 128), 1)
    row = jnp.zeros((8, 128), jnp.int32)
    for u in range(UNITS):
        wanted = owner[tiles[1 - u // SLOTS, u % SLOTS]]
        mine.append(wanted)
        row = jnp.where(lane == u, wanted, row)
    req_v[0] = row

    pl.semaphore_wait(barrier, len(greet))

    def z_copy(way, step, c):
        sign = 1 - 2 * way
        index = (z - sign * step + NZ) % NZ
        ref = slabs.at[index, c // 2, pl.ds(c % 2 * GC, GC)]
        return pltpu.make_async_remote_copy(
            src_ref=ref, dst_ref=ref,
            send_sem=z_send.at[way, step, c], recv_sem=z_recv.at[way, step, c],
            device_id=at_z(sign), device_id_type=MESH,
        )

    def z_arrived(way, step, c):
        sign = 1 - 2 * way
        index = (z - sign * (step + 1) + NZ) % NZ
        ref = slabs.at[index, c // 2, pl.ds(c % 2 * GC, GC)]
        pltpu.make_async_remote_copy(
            src_ref=ref, dst_ref=ref,
            send_sem=z_send.at[way, step, c], recv_sem=z_recv.at[way, step, c],
            device_id=at_z(sign), device_id_type=MESH,
        ).wait_recv()

    last = NZ // 2 - 1

    def z_pieces(step):
        for c in range(CHUNKS):
            for way in (0, 1):
                if step < last or (c < CHUNKS // 2) == (way == 0):
                    yield way, c

    z_started = []
    for way, c in z_pieces(0):
        if (way, c) == (0, CHUNKS // 2):
            late.wait()
            transform(1)
        copy = z_copy(way, 0, c)
        copy.start()
        z_started.append(copy)

    r_copies = []
    for d in (1, 2, 3):
        copy = pltpu.make_async_remote_copy(
            src_ref=req_v.at[0], dst_ref=req_v.at[d],
            send_sem=r_send.at[d], recv_sem=r_recv.at[d],
            device_id=at_y(d), device_id_type=MESH,
        )
        copy.start()
        r_copies.append(copy)

    def fetch_requests():
        for copy in r_copies:
            copy.wait()
        local = [
            pltpu.make_async_copy(req_v.at[d], req_s.at[d], r_loc.at[d]) for d in (1, 2, 3)
        ]
        for copy in local:
            copy.start()
        for copy in local:
            copy.wait()

    for step in range(1, last + 1):
        for way, c in z_pieces(step):
            z_arrived(way, step - 1, c)
            copy = z_copy(way, step, c)
            copy.start()
            z_started.append(copy)
        if step == 4:
            fetch_requests()
        if step == last:
            for c in range(CHUNKS):
                for way in (0, 1):
                    if (way, c) not in list(z_pieces(last)):
                        z_arrived(way, step - 1, c)
    for way, c in z_pieces(last):
        z_arrived(way, last, c)

    def asked(d, u):
        wanted = mine[u] if d == 0 else req_s[(NY - d) % NY, 0, u]
        return wanted // NY, wanted % NY

    def send(src, dst, s_sem, r_sem, who):
        copy = pltpu.make_async_remote_copy(
            src_ref=src, dst_ref=dst, send_sem=s_sem, recv_sem=r_sem,
            device_id=who, device_id_type=MESH,
        )
        copy.start()
        return copy

    copies = {}
    eye = identity(BLOCK)

    def first_hop(u):
        index, _ = asked(2, u)
        for s in (0, 1):
            stage_a[u, s] = slabs[index, s]
            copies["a", u, s] = send(
                stage_a.at[u, s], got_x.at[u, s], a_send.at[u, s], a_recv.at[u, s],
                at_y(1 if s == 0 else -1),
            )

    def direct(u):
        for s, d, got in ((1, 1, got_p), (0, -1, got_m)):
            index, _ = asked(d % NY, u)
            stage_d[u, s] = slabs[index, s]
            copies["d", u, s] = send(
                stage_d.at[u, s], got.at[u, s], d_send.at[u, s], d_recv.at[u, s], at_y(d)
            )

    def merged(u):
        for s, d, got in ((0, 1, got_p), (1, -1, got_m)):
            index, column = asked(d % NY, u)
            copies["a", u, s].wait_recv()
            stage_m[u, s] = jnp.where(column == y, slabs[index, s], got_x[u, s])
            copies["m", u, s] = send(
                stage_m.at[u, s], got.at[u, s], m_send.at[u, s], m_recv.at[u, s], at_y(d)
            )

    def finish(u):
        index, column = asked(0, u)
        for s in (0, 1):
            copies["d", u, s].wait_recv()
            copies["m", u, s].wait_recv()
        up, down = (y + 1) % NY, (y + NY - 1) % NY
        own = column == y
        low = jnp.where(column == up, got_m[u, 0], got_p[u, 0])
        low = jnp.where(own, slabs[index, 0], low)
        high = jnp.where(column == down, got_p[u, 1], got_m[u, 1])
        high = jnp.where(own, slabs[index, 1], high)
        return low, high

    def send_first(k, value):
        for seg in (0, 1):
            turned = nt_dot(eye, value[seg].reshape(2 * NF, BLOCK)).astype(BF)
            packed[k, :, seg] = turned.reshape(NTM, 16, 2 * NF)
        for d in range(1, NTM):
            to = (t + d) % NTM
            copies["p", k, d] = send(
                packed.at[k, to], p_out.at[t, k], p_send.at[k, d], p_recv.at[k, d], at_t(d)
            )
        copies["p", k, 0] = pltpu.make_async_copy(
            packed.at[k, t], p_out.at[t, k], own_sem.at[SLOTS + k]
        )
        copies["p", k, 0].start()

    half = NG // 2

    def t_of(step, c=None):
        return ((x + step + NX) % NX) * 2 + (core if c is None else c)

    def b_send_to(k, n, src, where, who):
        copies["b", k, n] = send(src, where, b_send.at[k, n], b_recv.at[k, n], who)

    def b_arrived(k, n, ref):
        pltpu.make_async_remote_copy(
            src_ref=ref, dst_ref=ref, send_sem=b_send.at[k, n], recv_sem=b_recv.at[k, n],
            device_id=sibling, device_id_type=MESH,
        ).wait_recv()

    def send_second(k, value):
        picks[k, :, 0], picks[k, :, 1] = value
        mine_ref = picks.at[k]
        b_send_to(k, 0, mine_ref, b_out.at[k, t], at_x(1))
        b_send_to(k, 1, mine_ref, b_out.at[k, t], at_x(-1))
        b_send_to(k, 2, mine_ref, b_out.at[k, t], sibling)
        copies["o", k] = pltpu.make_async_copy(mine_ref, b_out.at[k, t], own_sem.at[k])
        copies["o", k].start()

    lower, upper = pl.ds(0, half), pl.ds(half, half)

    def pass_second(k):
        low = b_out.at[k, t_of(-1)]
        b_arrived(k, 0, low)
        b_send_to(k, 3, b_out.at[k, t_of(-1), lower], b_out.at[k, t_of(-1), lower], at_x(1))
        b_send_to(k, 5, low, low, sibling)
        high = b_out.at[k, t_of(1)]
        b_arrived(k, 1, high)
        b_send_to(k, 4, b_out.at[k, t_of(1), upper], b_out.at[k, t_of(1), upper], at_x(-1))
        b_send_to(k, 6, high, high, sibling)

    def share_second(k):
        far_low = b_out.at[k, t_of(2), lower]
        b_arrived(k, 3, far_low)
        b_send_to(k, 7, far_low, far_low, sibling)
        far_up = b_out.at[k, t_of(2), upper]
        b_arrived(k, 4, far_up)
        b_send_to(k, 8, far_up, far_up, sibling)

    def close_second(k):
        b_arrived(k, 2, b_out.at[k, t_of(0, 1 - core)])
        b_arrived(k, 5, b_out.at[k, t_of(-1, 1 - core)])
        b_arrived(k, 6, b_out.at[k, t_of(1, 1 - core)])
        b_arrived(k, 7, b_out.at[k, t_of(2, 1 - core), lower])
        b_arrived(k, 8, b_out.at[k, t_of(2, 1 - core), upper])

    first_hop(0)
    first_hop(1)
    direct(0)
    for u in range(UNITS + 1):
        if u < UNITS:
            merged(u)
            if u + 2 < UNITS:
                first_hop(u + 2)
            if u + 1 < UNITS:
                direct(u + 1)
        if u == 0:
            continue
        value = finish(u - 1)
        if u - 1 < SLOTS:
            send_second(u - 1, value)
        else:
            send_first(u - 1 - SLOTS, value)
        if 0 <= u - 2 < SLOTS:
            pass_second(u - 2)
        if 0 <= u - 3 < SLOTS:
            share_second(u - 3)
    for k in range(SLOTS):
        close_second(k)
        copies["o", k].wait()
    for k in range(SLOTS):
        for d in range(1, NTM):
            come = (t + NTM - d) % NTM
            pltpu.make_async_remote_copy(
                src_ref=packed.at[k, 0], dst_ref=p_out.at[come, k],
                send_sem=p_send.at[k, d], recv_sem=p_recv.at[k, d],
                device_id=sibling, device_id_type=MESH,
            ).wait_recv()
        copies["p", k, 0].wait()
    for copy in z_started:
        copy.wait_send()
    for u in range(UNITS):
        for s in (0, 1):
            for kind in ("a", "d", "m"):
                copies[kind, u, s].wait_send()
    for k in range(SLOTS):
        for d in range(1, NTM):
            copies["p", k, d].wait_send()
        for n in range(9):
            copies["b", k, n].wait_send()


def exchange(traces, owner, tiles):
    seg_count = traces.shape[0]
    rows = seg_count * BLOCK
    tab_hi, tab_lo = forward_table()
    hbm = pl.BlockSpec(memory_space=pltpu.HBM)
    anywhere = pl.BlockSpec(memory_space=pl.ANY)
    half_units = (UNITS, 2, NG, 16, BLOCK)
    dma = pltpu.SemaphoreType.DMA
    return pl.pallas_call(
        exchange_kernel,
        out_shape=(
            jax.ShapeDtypeStruct((SLOTS, NTM, NG, 2, 16, BLOCK), BF),
            jax.ShapeDtypeStruct((NTM, SLOTS, 2, 16, 2 * NF), BF),
        ),
        in_specs=[hbm, hbm, hbm, hbm, hbm],
        out_specs=(anywhere, anywhere),
        scratch_shapes=[
            pltpu.SMEM(owner.shape, jnp.int32),
            pltpu.SMEM(tiles.shape[::-1], jnp.int32),
            pltpu.VMEM((rows, NT), F32),
            pltpu.VMEM((2 * NF, NT), BF),
            pltpu.VMEM((2 * NF, NT), BF),
            dma((6,)),
            pltpu.VMEM((NZ, 2, NG, 16, BLOCK), BF),
            pltpu.VMEM((SLOTS, NG, 2, 16, BLOCK), BF),
            pltpu.VMEM(half_units, BF),
            pltpu.VMEM(half_units, BF),
            pltpu.VMEM(half_units, BF),
            pltpu.VMEM(half_units, BF),
            pltpu.VMEM(half_units, BF),
            pltpu.VMEM(half_units, BF),
            pltpu.VMEM((SLOTS, NTM, 2, 16, 2 * NF), BF),
            pltpu.VMEM((NY, 8, 128), jnp.int32),
            pltpu.SMEM((NY, 8, 128), jnp.int32),
            dma((2, NZ // 2, CHUNKS)), dma((2, NZ // 2, CHUNKS)),
            dma((NY,)), dma((NY,)), dma((NY,)),
            dma((UNITS, 2)), dma((UNITS, 2)),
            dma((UNITS, 2)), dma((UNITS, 2)),
            dma((UNITS, 2)), dma((UNITS, 2)),
            dma((SLOTS, 9)), dma((SLOTS, 9)),
            dma((SLOTS, NTM)), dma((SLOTS, NTM)),
            dma((2 * SLOTS,)),
        ],
        compiler_params=pltpu.CompilerParams(
            collective_id=0, has_side_effects=True, vmem_limit_bytes=48 << 20
        ),
        name="exchange",
    )(*[in_hbm(a) for a in (traces.reshape(rows, NT), tab_hi, tab_lo, owner, tiles.T)])


def stack_kernel(scale, counts, p_ref, b_ref, inv_hi, inv_lo, out, natural, first, turned, high, low):
    k = pl.program_id(0)

    @pl.when(k == 0)
    def _():
        eye = identity(2 * NF)
        used = SLOTS * 32
        pad = jnp.zeros((2 * NF, BLOCK - used), BF)
        for t in range(NTM):
            back = nt_dot(eye, p_ref[t].reshape(used, 2 * NF)).astype(BF)
            natural[t] = jnp.concatenate([back, pad], axis=1)
        eye = identity(BLOCK)
        for g in range(NG):
            tile = natural[:, g * 16 : (g + 1) * 16, :]
            first[g] = nt_dot(eye, tile.reshape(BLOCK, BLOCK))
            wide = tile.astype(F32)
            wide = jnp.concatenate([-wide[:, 8:], wide[:, :8]], axis=1)
            turned[g] = nt_dot(eye, wide.astype(BF).reshape(BLOCK, BLOCK))

    shape = (8, BLOCK)
    mask = lax.broadcasted_iota(jnp.int32, shape, 1) % 8 == lax.broadcasted_iota(
        jnp.int32, shape, 0
    )
    mask = jnp.where(mask, 1.0, 0.0).astype(F32)[None]

    def group(g):
        halves = []
        for s in (0, 1):
            rows = pl.ds(pl.multiple_of(k * 32 + s * 16, 16), 16)
            direct = first[g, rows, :][:, None, :] * mask
            crossed = turned[g, rows, :][:, None, :] * mask
            both = jnp.concatenate([direct, crossed], axis=1).astype(BF)
            halves.append(both.reshape(2 * NF, BLOCK))
        lhs = jnp.concatenate(halves, axis=1)
        rhs = jnp.concatenate([b_ref[k, t, g, s] for s in (0, 1) for t in range(NTM)], axis=0)
        cross = jnp.dot(lhs, rhs, preferred_element_type=F32).reshape(16, 16, BLOCK)
        rows = slice(g * 16, g * 16 + 16)
        top = cross.astype(BF)
        high[:, rows, :] = top
        low[:, rows, :] = (cross - top.astype(F32)).astype(BF)

    for g in range(NG):
        group(g)
    factor = jnp.where(k < counts[0], scale, 0.0)
    for i in range(0, 16, 2):
        c_hi = jnp.concatenate([high[i], high[i + 1]], axis=1)
        c_lo = jnp.concatenate([low[i], low[i + 1]], axis=1)
        lagged = jnp.dot(inv_hi[...], c_hi, preferred_element_type=F32)
        lagged = lagged + jnp.dot(inv_lo[...], c_hi, preferred_element_type=F32)
        lagged = lagged + jnp.dot(inv_hi[...], c_lo, preferred_element_type=F32)
        out[:, i * BLOCK : (i + 2) * BLOCK] = lagged * factor


def stack(counts, p_all, b_all, scale):
    inv_hi, inv_lo = inverse_table()
    share = BLOCK // NTM
    return pl.pallas_call(
        functools.partial(stack_kernel, scale),
        grid=(SLOTS,),
        out_shape=jax.ShapeDtypeStruct((SLOTS, LAGS, share * BLOCK), F32),
        in_specs=[
            pl.BlockSpec(memory_space=pltpu.SMEM),
            pl.BlockSpec(memory_space=pltpu.VMEM),
            pl.BlockSpec(memory_space=pltpu.VMEM),
            pl.BlockSpec((LAGS, 2 * NF), lambda k: (0, 0)),
            pl.BlockSpec((LAGS, 2 * NF), lambda k: (0, 0)),
        ],
        out_specs=pl.BlockSpec((None, LAGS, share * BLOCK), lambda k: (k, 0, 0)),
        scratch_shapes=[
            pltpu.VMEM((NTM, 2 * NF, BLOCK), BF),
            pltpu.VMEM((NG, BLOCK, BLOCK), F32),
            pltpu.VMEM((NG, BLOCK, BLOCK), F32),
            pltpu.VMEM((16, 2 * NF, BLOCK), BF),
            pltpu.VMEM((16, 2 * NF, BLOCK), BF),
        ],
        compiler_params=pltpu.CompilerParams(
            dimension_semantics=("arbitrary",), vmem_limit_bytes=32 << 20
        ),
        name="stack",
    )(counts, p_all, b_all, in_hbm(inv_hi), in_hbm(inv_lo))


def shards(traces, owner, tiles, counts):
    segments = traces.shape[0] * NTM
    b_all, p_all = exchange(traces, owner, tiles)
    return stack(counts, p_all, b_all, 1.0 / math.sqrt(segments * NF))


def solution(mesh):
    placed = (P("tm", "pair", None), P(), P("pair", None), P("pair"))
    return jax.shard_map(
        shards, mesh=mesh, in_specs=placed, out_specs=P("pair", None, "tm"), check_vma=False
    )
```

```python
import functools
import math

import jax
import jax.numpy as jnp
import ml_dtypes
import numpy as np
from jax import lax
from jax.experimental import pallas as pl
from jax.experimental.pallas import tpu as pltpu
from jax.sharding import PartitionSpec as P

BLOCK = 128
NT = 1024
NF = 128
LOW_BIN = 8
LAGS = 128
NG = 16
NZ = 16
NY = 4
NX = 4
NTM = 8
SLOTS = 3
UNITS = 2 * SLOTS
CHUNKS = 4
GC = 2 * NG // CHUNKS
BF = jnp.bfloat16
F32 = jnp.float32
MESH = pl.DeviceIdType.MESH


def split(table):
    high = table.astype(np.float32).astype(ml_dtypes.bfloat16)
    low = (table.astype(np.float32) - high.astype(np.float32)).astype(ml_dtypes.bfloat16)
    return high, low


def forward_table():
    samples = np.arange(NT)
    bins = LOW_BIN + np.arange(NF)
    angle = (bins[:, None] * samples[None, :] % NT) * (2.0 * math.pi / NT)
    return split(np.concatenate([np.cos(angle), -np.sin(angle)], axis=0))


def inverse_table():
    shifts = np.arange(LAGS) - LAGS // 2
    bins = LOW_BIN + np.arange(NF)
    angle = (shifts[:, None] * bins[None, :] % NT) * (2.0 * math.pi / NT)
    parts = np.stack([np.cos(angle), -np.sin(angle)], axis=0)
    parts = parts.reshape(2, LAGS, NG, 8).transpose(1, 2, 0, 3)
    return split(parts.reshape(LAGS, 2 * NF))


def in_hbm(array):
    return pltpu.with_memory_space_constraint(jnp.asarray(array), pltpu.HBM)


def nt_dot(a, b):
    return lax.dot_general(a, b, (((1,), (1,)), ((), ())), preferred_element_type=F32)


def identity(size):
    row = lax.broadcasted_iota(jnp.int32, (size, size), 0)
    return jnp.where(row == lax.broadcasted_iota(jnp.int32, (size, size), 1), 1.0, 0.0).astype(BF)


def exchange_kernel(
    traces_hbm, hi_hbm, lo_hbm, owner_hbm, tiles_hbm, b_out, p_out,
    owner, tiles, traces, tab_hi, tab_lo, load_sem, slabs, picks, stage_a, stage_d, stage_m, got_x, got_p, got_m,
    packed, req_v, req_s,
    z_send, z_recv, r_send, r_recv, r_loc, a_send, a_recv, d_send, d_recv, m_send, m_recv,
    b_send, b_recv, p_send, p_recv, own_sem,
):
    t = lax.axis_index("tm")
    pair = lax.axis_index("pair")
    z, y = pair // NY, pair % NY
    x, core = t // 2, t % 2

    def at_z(step):
        return {"pair": ((z + step + NZ) % NZ) * NY + y}

    def at_y(step):
        return {"pair": z * NY + (y + step + NY) % NY}

    def at_x(step):
        return {"tm": ((x + step + NX) % NX) * 2 + core}

    def at_t(step):
        return {"tm": (t + step) % NTM}

    sibling = {"tm": x * 2 + 1 - core}

    barrier = pltpu.get_barrier_semaphore()
    greet = [at_z(1), at_z(-1)] + [at_y(d) for d in (1, 2, 3)] + [at_t(d) for d in range(1, NTM)]
    for who in greet:
        pl.semaphore_signal(barrier, inc=1, device_id=who, device_id_type=MESH)

    def load(n, src, dst):
        copy = pltpu.make_async_copy(src, dst, load_sem.at[n])
        copy.start()
        return copy

    rows = [pl.ds(seg * BLOCK, BLOCK) for seg in (0, 1)]
    early = [
        load(0, owner_hbm, owner), load(1, tiles_hbm, tiles),
        load(2, traces_hbm.at[rows[0]], traces.at[rows[0]]),
        load(3, hi_hbm, tab_hi), load(4, lo_hbm, tab_lo),
    ]
    late = load(5, traces_hbm.at[rows[1]], traces.at[rows[1]])
    for copy in early:
        copy.wait()

    def transform(seg):
        values = traces[rows[seg], :]
        v_hi = values.astype(BF)
        v_lo = (values - v_hi.astype(F32)).astype(BF)
        spec = nt_dot(tab_hi[...], v_hi) + (nt_dot(tab_hi[...], v_lo) + nt_dot(tab_lo[...], v_hi))
        real, imag = spec[:NF], spec[NF:]
        power = real * real + imag * imag
        bin_of = lax.broadcasted_iota(jnp.int32, power.shape, 0)
        total = power
        for step in (1, 2):
            ahead = pltpu.roll(power, NF - step, 0)
            behind = pltpu.roll(power, step, 0)
            total = total + jnp.where(bin_of < NF - step, ahead, 0.0)
            total = total + jnp.where(bin_of >= step, behind, 0.0)
        edge = jnp.minimum(jnp.minimum(bin_of, NF - 1 - bin_of), 2)
        smooth = total / (edge + 3).astype(F32)
        level = jnp.sum(power, axis=0, keepdims=True) * (1.0 / NF)
        factor = lax.rsqrt(smooth + 0.05 * level + 1e-06)
        slabs[z, seg] = jnp.concatenate(
            [(real * factor).reshape(NG, 8, BLOCK), (imag * factor).reshape(NG, 8, BLOCK)], axis=1
        ).astype(BF)

    transform(0)

    mine = []
    lane = lax.broadcasted_iota(jnp.int32, (8, 128), 1)
    row = jnp.zeros((8, 128), jnp.int32)
    for u in range(UNITS):
        wanted = owner[tiles[1 - u // SLOTS, u % SLOTS]]
        mine.append(wanted)
        row = jnp.where(lane == u, wanted, row)
    req_v[0] = row

    pl.semaphore_wait(barrier, len(greet))

    def z_copy(way, step, c):
        sign = 1 - 2 * way
        index = (z - sign * step + NZ) % NZ
        ref = slabs.at[index, c // 2, pl.ds(c % 2 * GC, GC)]
        return pltpu.make_async_remote_copy(
            src_ref=ref, dst_ref=ref,
            send_sem=z_send.at[way, step, c], recv_sem=z_recv.at[way, step, c],
            device_id=at_z(sign), device_id_type=MESH,
        )

    def z_arrived(way, step, c):
        sign = 1 - 2 * way
        index = (z - sign * (step + 1) + NZ) % NZ
        ref = slabs.at[index, c // 2, pl.ds(c % 2 * GC, GC)]
        pltpu.make_async_remote_copy(
            src_ref=ref, dst_ref=ref,
            send_sem=z_send.at[way, step, c], recv_sem=z_recv.at[way, step, c],
            device_id=at_z(sign), device_id_type=MESH,
        ).wait_recv()

    last = NZ // 2 - 1

    def z_pieces(step):
        for c in range(CHUNKS):
            for way in (0, 1):
                if step < last or (c < CHUNKS // 2) == (way == 0):
                    yield way, c

    z_started = []
    for way, c in z_pieces(0):
        if (way, c) == (0, CHUNKS // 2):
            late.wait()
            transform(1)
        copy = z_copy(way, 0, c)
        copy.start()
        z_started.append(copy)

    r_copies = []
    for d in (1, 2, 3):
        copy = pltpu.make_async_remote_copy(
            src_ref=req_v.at[0], dst_ref=req_v.at[d],
            send_sem=r_send.at[d], recv_sem=r_recv.at[d],
            device_id=at_y(d), device_id_type=MESH,
        )
        copy.start()
        r_copies.append(copy)

    def fetch_requests():
        for copy in r_copies:
            copy.wait()
        local = [
            pltpu.make_async_copy(req_v.at[d], req_s.at[d], r_loc.at[d]) for d in (1, 2, 3)
        ]
        for copy in local:
            copy.start()
        for copy in local:
            copy.wait()

    for step in range(1, last + 1):
        for way, c in z_pieces(step):
            z_arrived(way, step - 1, c)
            copy = z_copy(way, step, c)
            copy.start()
            z_started.append(copy)
        if step == 4:
            fetch_requests()
        if step == last:
            for c in range(CHUNKS):
                for way in (0, 1):
                    if (way, c) not in list(z_pieces(last)):
                        z_arrived(way, step - 1, c)
    for way, c in z_pieces(last):
        z_arrived(way, last, c)

    def asked(d, u):
        wanted = mine[u] if d == 0 else req_s[(NY - d) % NY, 0, u]
        return wanted // NY, wanted % NY

    def send(src, dst, s_sem, r_sem, who):
        copy = pltpu.make_async_remote_copy(
            src_ref=src, dst_ref=dst, send_sem=s_sem, recv_sem=r_sem,
            device_id=who, device_id_type=MESH,
        )
        copy.start()
        return copy

    copies = {}
    eye = identity(BLOCK)

    def first_hop(u):
        index, _ = asked(2, u)
        for s in (0, 1):
            stage_a[u, s] = slabs[index, s]
            copies["a", u, s] = send(
                stage_a.at[u, s], got_x.at[u, s], a_send.at[u, s], a_recv.at[u, s],
                at_y(1 if s == 0 else -1),
            )

    def direct(u):
        for s, d, got in ((1, 1, got_p), (0, -1, got_m)):
            index, _ = asked(d % NY, u)
            stage_d[u, s] = slabs[index, s]
            copies["d", u, s] = send(
                stage_d.at[u, s], got.at[u, s], d_send.at[u, s], d_recv.at[u, s], at_y(d)
            )

    def merged(u):
        for s, d, got in ((0, 1, got_p), (1, -1, got_m)):
            index, column = asked(d % NY, u)
            copies["a", u, s].wait_recv()
            stage_m[u, s] = jnp.where(column == y, slabs[index, s], got_x[u, s])
            copies["m", u, s] = send(
                stage_m.at[u, s], got.at[u, s], m_send.at[u, s], m_recv.at[u, s], at_y(d)
            )

    def finish(u):
        index, column = asked(0, u)
        for s in (0, 1):
            copies["d", u, s].wait_recv()
            copies["m", u, s].wait_recv()
        up, down = (y + 1) % NY, (y + NY - 1) % NY
        own = column == y
        low = jnp.where(column == up, got_m[u, 0], got_p[u, 0])
        low = jnp.where(own, slabs[index, 0], low)
        high = jnp.where(column == down, got_p[u, 1], got_m[u, 1])
        high = jnp.where(own, slabs[index, 1], high)
        return low, high

    def send_first(k, value):
        for seg in (0, 1):
            turned = nt_dot(eye, value[seg].reshape(2 * NF, BLOCK)).astype(BF)
            packed[k, :, seg] = turned.reshape(NTM, 16, 2 * NF)
        for d in range(1, NTM):
            to = (t + d) % NTM
            copies["p", k, d] = send(
                packed.at[k, to], p_out.at[t, k], p_send.at[k, d], p_recv.at[k, d], at_t(d)
            )
        copies["p", k, 0] = pltpu.make_async_copy(
            packed.at[k, t], p_out.at[t, k], own_sem.at[SLOTS + k]
        )
        copies["p", k, 0].start()

    half = NG // 2

    def t_of(step, c=None):
        return ((x + step + NX) % NX) * 2 + (core if c is None else c)

    def b_send_to(k, n, src, where, who):
        copies["b", k, n] = send(src, where, b_send.at[k, n], b_recv.at[k, n], who)

    def b_arrived(k, n, ref):
        pltpu.make_async_remote_copy(
            src_ref=ref, dst_ref=ref, send_sem=b_send.at[k, n], recv_sem=b_recv.at[k, n],
            device_id=sibling, device_id_type=MESH,
        ).wait_recv()

    def send_second(k, value):
        picks[k, :, 0], picks[k, :, 1] = value
        mine_ref = picks.at[k]
        b_send_to(k, 0, mine_ref, b_out.at[k, t], at_x(1))
        b_send_to(k, 1, mine_ref, b_out.at[k, t], at_x(-1))
        b_send_to(k, 2, mine_ref, b_out.at[k, t], sibling)
        copies["o", k] = pltpu.make_async_copy(mine_ref, b_out.at[k, t], own_sem.at[k])
        copies["o", k].start()

    lower, upper = pl.ds(0, half), pl.ds(half, half)

    def pass_second(k):
        low = b_out.at[k, t_of(-1)]
        b_arrived(k, 0, low)
        b_send_to(k, 3, b_out.at[k, t_of(-1), lower], b_out.at[k, t_of(-1), lower], at_x(1))
        b_send_to(k, 5, low, low, sibling)
        high = b_out.at[k, t_of(1)]
        b_arrived(k, 1, high)
        b_send_to(k, 4, b_out.at[k, t_of(1), upper], b_out.at[k, t_of(1), upper], at_x(-1))
        b_send_to(k, 6, high, high, sibling)

    def share_second(k):
        far_low = b_out.at[k, t_of(2), lower]
        b_arrived(k, 3, far_low)
        b_send_to(k, 7, far_low, far_low, sibling)
        far_up = b_out.at[k, t_of(2), upper]
        b_arrived(k, 4, far_up)
        b_send_to(k, 8, far_up, far_up, sibling)

    def close_second(k):
        b_arrived(k, 2, b_out.at[k, t_of(0, 1 - core)])
        b_arrived(k, 5, b_out.at[k, t_of(-1, 1 - core)])
        b_arrived(k, 6, b_out.at[k, t_of(1, 1 - core)])
        b_arrived(k, 7, b_out.at[k, t_of(2, 1 - core), lower])
        b_arrived(k, 8, b_out.at[k, t_of(2, 1 - core), upper])

    first_hop(0)
    first_hop(1)
    direct(0)
    for u in range(UNITS + 1):
        if u < UNITS:
            merged(u)
            if u + 2 < UNITS:
                first_hop(u + 2)
            if u + 1 < UNITS:
                direct(u + 1)
        if u == 0:
            continue
        value = finish(u - 1)
        if u - 1 < SLOTS:
            send_second(u - 1, value)
        else:
            send_first(u - 1 - SLOTS, value)
        if 0 <= u - 2 < SLOTS:
            pass_second(u - 2)
        if 0 <= u - 3 < SLOTS:
            share_second(u - 3)
    for k in range(SLOTS):
        close_second(k)
        copies["o", k].wait()
    for k in range(SLOTS):
        for d in range(1, NTM):
            come = (t + NTM - d) % NTM
            pltpu.make_async_remote_copy(
                src_ref=packed.at[k, 0], dst_ref=p_out.at[come, k],
                send_sem=p_send.at[k, d], recv_sem=p_recv.at[k, d],
                device_id=sibling, device_id_type=MESH,
            ).wait_recv()
        copies["p", k, 0].wait()
    for copy in z_started:
        copy.wait_send()
    for u in range(UNITS):
        for s in (0, 1):
            for kind in ("a", "d", "m"):
                copies[kind, u, s].wait_send()
    for k in range(SLOTS):
        for d in range(1, NTM):
            copies["p", k, d].wait_send()
        for n in range(9):
            copies["b", k, n].wait_send()


def exchange(traces, owner, tiles):
    seg_count = traces.shape[0]
    rows = seg_count * BLOCK
    tab_hi, tab_lo = forward_table()
    hbm = pl.BlockSpec(memory_space=pltpu.HBM)
    anywhere = pl.BlockSpec(memory_space=pl.ANY)
    half_units = (UNITS, 2, NG, 16, BLOCK)
    dma = pltpu.SemaphoreType.DMA
    return pl.pallas_call(
        exchange_kernel,
        out_shape=(
            jax.ShapeDtypeStruct((SLOTS, NTM, NG, 2, 16, BLOCK), BF),
            jax.ShapeDtypeStruct((NTM, SLOTS, 2, 16, 2 * NF), BF),
        ),
        in_specs=[hbm, hbm, hbm, hbm, hbm],
        out_specs=(anywhere, anywhere),
        scratch_shapes=[
            pltpu.SMEM(owner.shape, jnp.int32),
            pltpu.SMEM(tiles.shape[::-1], jnp.int32),
            pltpu.VMEM((rows, NT), F32),
            pltpu.VMEM((2 * NF, NT), BF),
            pltpu.VMEM((2 * NF, NT), BF),
            dma((6,)),
            pltpu.VMEM((NZ, 2, NG, 16, BLOCK), BF),
            pltpu.VMEM((SLOTS, NG, 2, 16, BLOCK), BF),
            pltpu.VMEM(half_units, BF),
            pltpu.VMEM(half_units, BF),
            pltpu.VMEM(half_units, BF),
            pltpu.VMEM(half_units, BF),
            pltpu.VMEM(half_units, BF),
            pltpu.VMEM(half_units, BF),
            pltpu.VMEM((SLOTS, NTM, 2, 16, 2 * NF), BF),
            pltpu.VMEM((NY, 8, 128), jnp.int32),
            pltpu.SMEM((NY, 8, 128), jnp.int32),
            dma((2, NZ // 2, CHUNKS)), dma((2, NZ // 2, CHUNKS)),
            dma((NY,)), dma((NY,)), dma((NY,)),
            dma((UNITS, 2)), dma((UNITS, 2)),
            dma((UNITS, 2)), dma((UNITS, 2)),
            dma((UNITS, 2)), dma((UNITS, 2)),
            dma((SLOTS, 9)), dma((SLOTS, 9)),
            dma((SLOTS, NTM)), dma((SLOTS, NTM)),
            dma((2 * SLOTS,)),
        ],
        compiler_params=pltpu.CompilerParams(
            collective_id=0, has_side_effects=True, vmem_limit_bytes=48 << 20
        ),
        name="exchange",
    )(*[in_hbm(a) for a in (traces.reshape(rows, NT), tab_hi, tab_lo, owner, tiles.T)])


def stack_kernel(
    scale, counts, p_ref, b_ref, hi_hbm, lo_hbm, out,
    inv_hi, inv_lo, natural, first, turned, high, low, result, load_sem, out_sem,
):
    loads = [
        pltpu.make_async_copy(hi_hbm, inv_hi, load_sem.at[0]),
        pltpu.make_async_copy(lo_hbm, inv_lo, load_sem.at[1]),
    ]
    for load in loads:
        load.start()

    eye = identity(2 * NF)
    used = SLOTS * 32
    pad = jnp.zeros((2 * NF, BLOCK - used), BF)
    for t in range(NTM):
        back = nt_dot(eye, p_ref[t].reshape(used, 2 * NF)).astype(BF)
        natural[t] = jnp.concatenate([back, pad], axis=1)
    eye = identity(BLOCK)
    for g in range(NG):
        tile = natural[:, g * 16 : (g + 1) * 16, :]
        first[g] = nt_dot(eye, tile.reshape(BLOCK, BLOCK))
        wide = tile.astype(F32)
        wide = jnp.concatenate([-wide[:, 8:], wide[:, :8]], axis=1)
        turned[g] = nt_dot(eye, wide.astype(BF).reshape(BLOCK, BLOCK))

    shape = (8, BLOCK)
    mask = lax.broadcasted_iota(jnp.int32, shape, 1) % 8 == lax.broadcasted_iota(
        jnp.int32, shape, 0
    )
    mask = jnp.where(mask, 1.0, 0.0).astype(F32)[None]

    def group(k, g):
        halves = []
        for s in (0, 1):
            rows = slice(k * 32 + s * 16, k * 32 + s * 16 + 16)
            direct = first[g, rows, :][:, None, :] * mask
            crossed = turned[g, rows, :][:, None, :] * mask
            both = jnp.concatenate([direct, crossed], axis=1).astype(BF)
            halves.append(both.reshape(2 * NF, BLOCK))
        lhs = jnp.concatenate(halves, axis=1)
        rhs = jnp.concatenate([b_ref[k, t, g, s] for s in (0, 1) for t in range(NTM)], axis=0)
        cross = jnp.dot(lhs, rhs, preferred_element_type=F32).reshape(16, 16, BLOCK)
        rows = slice(g * 16, g * 16 + 16)
        top = cross.astype(BF)
        high[k, :, rows, :] = top
        low[k, :, rows, :] = (cross - top.astype(F32)).astype(BF)

    copies = []
    for k in range(SLOTS):
        for g in range(NG):
            group(k, g)
        if k == 0:
            for load in loads:
                load.wait()
        factor = jnp.where(k < counts[0], scale, 0.0)
        for i in range(0, 16, 2):
            c_hi = jnp.concatenate([high[k, i], high[k, i + 1]], axis=1)
            c_lo = jnp.concatenate([low[k, i], low[k, i + 1]], axis=1)
            lagged = jnp.dot(inv_hi[...], c_hi, preferred_element_type=F32)
            lagged = lagged + jnp.dot(inv_lo[...], c_hi, preferred_element_type=F32)
            lagged = lagged + jnp.dot(inv_hi[...], c_lo, preferred_element_type=F32)
            result[k, :, i * BLOCK : (i + 2) * BLOCK] = lagged * factor
            if i % 8 == 6:
                lanes = pl.ds((i - 6) * BLOCK, 8 * BLOCK)
                copy = pltpu.make_async_copy(
                    result.at[k, :, lanes], out.at[k, :, lanes], out_sem.at[k, i // 8]
                )
                copy.start()
                copies.append(copy)
    for copy in copies:
        copy.wait()


def stack(counts, p_all, b_all, scale):
    inv_hi, inv_lo = inverse_table()
    share = BLOCK // NTM
    vmem = pl.BlockSpec(memory_space=pltpu.VMEM)
    hbm = pl.BlockSpec(memory_space=pltpu.HBM)
    return pl.pallas_call(
        functools.partial(stack_kernel, scale),
        out_shape=jax.ShapeDtypeStruct((SLOTS, LAGS, share * BLOCK), F32),
        in_specs=[pl.BlockSpec(memory_space=pltpu.SMEM), vmem, vmem, hbm, hbm],
        out_specs=hbm,
        scratch_shapes=[
            pltpu.VMEM((LAGS, 2 * NF), BF),
            pltpu.VMEM((LAGS, 2 * NF), BF),
            pltpu.VMEM((NTM, 2 * NF, BLOCK), BF),
            pltpu.VMEM((NG, BLOCK, BLOCK), F32),
            pltpu.VMEM((NG, BLOCK, BLOCK), F32),
            pltpu.VMEM((SLOTS, 16, 2 * NF, BLOCK), BF),
            pltpu.VMEM((SLOTS, 16, 2 * NF, BLOCK), BF),
            pltpu.VMEM((SLOTS, LAGS, share * BLOCK), F32),
            pltpu.SemaphoreType.DMA((2,)),
            pltpu.SemaphoreType.DMA((SLOTS, 2)),
        ],
        compiler_params=pltpu.CompilerParams(vmem_limit_bytes=32 << 20),
        name="stack",
    )(counts, p_all, b_all, in_hbm(inv_hi), in_hbm(inv_lo))


def shards(traces, owner, tiles, counts):
    segments = traces.shape[0] * NTM
    b_all, p_all = exchange(traces, owner, tiles)
    return stack(counts, p_all, b_all, 1.0 / math.sqrt(segments * NF))


def solution(mesh):
    placed = (P("tm", "pair", None), P(), P("pair", None), P("pair"))
    return jax.shard_map(
        shards, mesh=mesh, in_specs=placed, out_specs=P("pair", None, "tm"), check_vma=False
    )
```

```python
import functools
import math

import jax
import jax.numpy as jnp
import ml_dtypes
import numpy as np
from jax import lax
from jax.experimental import pallas as pl
from jax.experimental.pallas import tpu as pltpu
from jax.sharding import PartitionSpec as P

BLOCK = 128
NT = 1024
NF = 128
LOW_BIN = 8
LAGS = 128
NG = 16
NZ = 16
NY = 4
NX = 4
NTM = 8
SLOTS = 3
UNITS = 2 * SLOTS
CHUNKS = 4
GC = 2 * NG // CHUNKS
BF = jnp.bfloat16
F32 = jnp.float32
MESH = pl.DeviceIdType.MESH


def split(table):
    high = table.astype(np.float32).astype(ml_dtypes.bfloat16)
    low = (table.astype(np.float32) - high.astype(np.float32)).astype(ml_dtypes.bfloat16)
    return high, low


def forward_table():
    samples = np.arange(NT)
    bins = LOW_BIN + np.arange(NF)
    angle = (bins[:, None] * samples[None, :] % NT) * (2.0 * math.pi / NT)
    return split(np.concatenate([np.cos(angle), -np.sin(angle)], axis=0))


def inverse_table():
    shifts = np.arange(LAGS) - LAGS // 2
    bins = LOW_BIN + np.arange(NF)
    angle = (shifts[:, None] * bins[None, :] % NT) * (2.0 * math.pi / NT)
    parts = np.stack([np.cos(angle), -np.sin(angle)], axis=0)
    parts = parts.reshape(2, LAGS, NG, 8).transpose(1, 2, 0, 3)
    return split(parts.reshape(LAGS, 2 * NF))


def in_hbm(array):
    return pltpu.with_memory_space_constraint(jnp.asarray(array), pltpu.HBM)


def nt_dot(a, b):
    return lax.dot_general(a, b, (((1,), (1,)), ((), ())), preferred_element_type=F32)


def identity(size):
    row = lax.broadcasted_iota(jnp.int32, (size, size), 0)
    return jnp.where(row == lax.broadcasted_iota(jnp.int32, (size, size), 1), 1.0, 0.0).astype(BF)


def exchange_kernel(
    traces_hbm, hi_hbm, lo_hbm, owner_hbm, tiles_hbm, b_out, p_out,
    owner, tiles, traces, tab_hi, tab_lo, load_sem, slabs, picks, stage_a, stage_d, stage_m, got_x, got_p, got_m,
    packed, req_v, req_s,
    z_send, z_recv, r_send, r_recv, r_loc, a_send, a_recv, m_send, m_recv,
    b_send, b_recv, p_send, p_recv, own_sem,
):
    t = lax.axis_index("tm")
    pair = lax.axis_index("pair")
    z, y = pair // NY, pair % NY
    x, core = t // 2, t % 2

    def at_z(step):
        return {"pair": ((z + step + NZ) % NZ) * NY + y}

    def at_y(step):
        return {"pair": z * NY + (y + step + NY) % NY}

    def at_x(step):
        return {"tm": ((x + step + NX) % NX) * 2 + core}

    def at_t(step):
        return {"tm": (t + step) % NTM}

    sibling = {"tm": x * 2 + 1 - core}

    barrier = pltpu.get_barrier_semaphore()
    greet = [at_z(1), at_z(-1)] + [at_y(d) for d in (1, 2, 3)] + [at_t(d) for d in range(1, NTM)]
    for who in greet:
        pl.semaphore_signal(barrier, inc=1, device_id=who, device_id_type=MESH)

    def load(n, src, dst):
        copy = pltpu.make_async_copy(src, dst, load_sem.at[n])
        copy.start()
        return copy

    rows = [pl.ds(seg * BLOCK, BLOCK) for seg in (0, 1)]
    early = [
        load(0, owner_hbm, owner), load(1, tiles_hbm, tiles),
        load(2, traces_hbm.at[rows[0]], traces.at[rows[0]]),
        load(3, hi_hbm, tab_hi), load(4, lo_hbm, tab_lo),
    ]
    late = load(5, traces_hbm.at[rows[1]], traces.at[rows[1]])
    for copy in early:
        copy.wait()

    def transform(seg):
        values = traces[rows[seg], :]
        v_hi = values.astype(BF)
        v_lo = (values - v_hi.astype(F32)).astype(BF)
        spec = nt_dot(tab_hi[...], v_hi) + (nt_dot(tab_hi[...], v_lo) + nt_dot(tab_lo[...], v_hi))
        real, imag = spec[:NF], spec[NF:]
        power = real * real + imag * imag
        bin_of = lax.broadcasted_iota(jnp.int32, power.shape, 0)
        total = power
        for step in (1, 2):
            ahead = pltpu.roll(power, NF - step, 0)
            behind = pltpu.roll(power, step, 0)
            total = total + jnp.where(bin_of < NF - step, ahead, 0.0)
            total = total + jnp.where(bin_of >= step, behind, 0.0)
        edge = jnp.minimum(jnp.minimum(bin_of, NF - 1 - bin_of), 2)
        smooth = total / (edge + 3).astype(F32)
        level = jnp.sum(power, axis=0, keepdims=True) * (1.0 / NF)
        factor = lax.rsqrt(smooth + 0.05 * level + 1e-06)
        slabs[z, seg] = jnp.concatenate(
            [(real * factor).reshape(NG, 8, BLOCK), (imag * factor).reshape(NG, 8, BLOCK)], axis=1
        ).astype(BF)

    transform(0)

    mine = []
    lane = lax.broadcasted_iota(jnp.int32, (8, 128), 1)
    row = jnp.zeros((8, 128), jnp.int32)
    for u in range(UNITS):
        wanted = owner[tiles[1 - u // SLOTS, u % SLOTS]]
        mine.append(wanted)
        row = jnp.where(lane == u, wanted, row)
    req_v[0] = row

    pl.semaphore_wait(barrier, len(greet))

    def z_copy(way, step, c):
        sign = 1 - 2 * way
        index = (z - sign * step + NZ) % NZ
        ref = slabs.at[index, c // 2, pl.ds(c % 2 * GC, GC)]
        return pltpu.make_async_remote_copy(
            src_ref=ref, dst_ref=ref,
            send_sem=z_send.at[way, step, c], recv_sem=z_recv.at[way, step, c],
            device_id=at_z(sign), device_id_type=MESH,
        )

    def z_arrived(way, step, c):
        sign = 1 - 2 * way
        index = (z - sign * (step + 1) + NZ) % NZ
        ref = slabs.at[index, c // 2, pl.ds(c % 2 * GC, GC)]
        pltpu.make_async_remote_copy(
            src_ref=ref, dst_ref=ref,
            send_sem=z_send.at[way, step, c], recv_sem=z_recv.at[way, step, c],
            device_id=at_z(sign), device_id_type=MESH,
        ).wait_recv()

    last = NZ // 2 - 1

    def z_pieces(step):
        for c in range(CHUNKS):
            for way in (0, 1):
                if step < last or (c < CHUNKS // 2) == (way == 0):
                    yield way, c

    z_started = []
    for way, c in z_pieces(0):
        if (way, c) == (0, CHUNKS // 2):
            late.wait()
            transform(1)
        copy = z_copy(way, 0, c)
        copy.start()
        z_started.append(copy)

    r_copies = []
    for d in (1, 2, 3):
        copy = pltpu.make_async_remote_copy(
            src_ref=req_v.at[0], dst_ref=req_v.at[d],
            send_sem=r_send.at[d], recv_sem=r_recv.at[d],
            device_id=at_y(d), device_id_type=MESH,
        )
        copy.start()
        r_copies.append(copy)

    def fetch_requests():
        for copy in r_copies:
            copy.wait()
        local = [
            pltpu.make_async_copy(req_v.at[d], req_s.at[d], r_loc.at[d]) for d in (1, 2, 3)
        ]
        for copy in local:
            copy.start()
        for copy in local:
            copy.wait()

    for step in range(1, last + 1):
        for way, c in z_pieces(step):
            z_arrived(way, step - 1, c)
            copy = z_copy(way, step, c)
            copy.start()
            z_started.append(copy)
        if step == 4:
            fetch_requests()
        if step == last:
            for c in range(CHUNKS):
                for way in (0, 1):
                    if (way, c) not in list(z_pieces(last)):
                        z_arrived(way, step - 1, c)
    for way, c in z_pieces(last):
        z_arrived(way, last, c)

    def asked(d, u):
        wanted = mine[u] if d == 0 else req_s[(NY - d) % NY, 0, u]
        return wanted // NY, wanted % NY

    def send(src, dst, s_sem, r_sem, who):
        copy = pltpu.make_async_remote_copy(
            src_ref=src, dst_ref=dst, send_sem=s_sem, recv_sem=r_sem,
            device_id=who, device_id_type=MESH,
        )
        copy.start()
        return copy

    copies = {}
    eye = identity(BLOCK)

    def first_hop(u):
        index, _ = asked(2, u)
        for s in (0, 1):
            stage_a[u, s] = slabs[index, s]
            copies["a", u, s] = send(
                stage_a.at[u, s], got_x.at[u, s], a_send.at[u, s], a_recv.at[u, s],
                at_y(1 if s == 0 else -1),
            )

    def second_hop(u):
        for s, d, stage, got in ((0, 1, stage_d, got_p), (1, -1, stage_m, got_m)):
            index, column = asked(d % NY, u)
            stage[u, 1 - s] = slabs[index, 1 - s]
            copies["a", u, s].wait_recv()
            stage[u, s] = jnp.where(column == y, slabs[index, s], got_x[u, s])
            copies["m", u, s] = send(
                stage.at[u], got.at[u], m_send.at[u, s], m_recv.at[u, s], at_y(d)
            )

    def finish(u):
        index, column = asked(0, u)
        for s in (0, 1):
            copies["m", u, s].wait_recv()
        up, down = (y + 1) % NY, (y + NY - 1) % NY
        own = column == y
        low = jnp.where(column == up, got_m[u, 0], got_p[u, 0])
        low = jnp.where(own, slabs[index, 0], low)
        high = jnp.where(column == down, got_p[u, 1], got_m[u, 1])
        high = jnp.where(own, slabs[index, 1], high)
        return low, high

    def send_first(k, value):
        for seg in (0, 1):
            turned = nt_dot(eye, value[seg].reshape(2 * NF, BLOCK)).astype(BF)
            packed[k, :, seg] = turned.reshape(NTM, 16, 2 * NF)
        for d in range(1, NTM):
            to = (t + d) % NTM
            copies["p", k, d] = send(
                packed.at[k, to], p_out.at[t, k], p_send.at[k, d], p_recv.at[k, d], at_t(d)
            )
        copies["p", k, 0] = pltpu.make_async_copy(
            packed.at[k, t], p_out.at[t, k], own_sem.at[SLOTS + k]
        )
        copies["p", k, 0].start()

    half = NG // 2

    def t_of(step, c=None):
        return ((x + step + NX) % NX) * 2 + (core if c is None else c)

    def b_send_to(k, n, src, where, who):
        copies["b", k, n] = send(src, where, b_send.at[k, n], b_recv.at[k, n], who)

    def b_arrived(k, n, ref):
        pltpu.make_async_remote_copy(
            src_ref=ref, dst_ref=ref, send_sem=b_send.at[k, n], recv_sem=b_recv.at[k, n],
            device_id=sibling, device_id_type=MESH,
        ).wait_recv()

    def send_second(k, value):
        picks[k, :, 0], picks[k, :, 1] = value
        mine_ref = picks.at[k]
        b_send_to(k, 0, mine_ref, b_out.at[k, t], at_x(1))
        b_send_to(k, 1, mine_ref, b_out.at[k, t], at_x(-1))
        b_send_to(k, 2, mine_ref, b_out.at[k, t], sibling)
        copies["o", k] = pltpu.make_async_copy(mine_ref, b_out.at[k, t], own_sem.at[k])
        copies["o", k].start()

    lower, upper = pl.ds(0, half), pl.ds(half, half)

    def pass_second(k):
        low = b_out.at[k, t_of(-1)]
        b_arrived(k, 0, low)
        b_send_to(k, 3, b_out.at[k, t_of(-1), lower], b_out.at[k, t_of(-1), lower], at_x(1))
        b_send_to(k, 5, low, low, sibling)
        high = b_out.at[k, t_of(1)]
        b_arrived(k, 1, high)
        b_send_to(k, 4, b_out.at[k, t_of(1), upper], b_out.at[k, t_of(1), upper], at_x(-1))
        b_send_to(k, 6, high, high, sibling)

    def share_second(k):
        far_low = b_out.at[k, t_of(2), lower]
        b_arrived(k, 3, far_low)
        b_send_to(k, 7, far_low, far_low, sibling)
        far_up = b_out.at[k, t_of(2), upper]
        b_arrived(k, 4, far_up)
        b_send_to(k, 8, far_up, far_up, sibling)

    def close_second(k):
        b_arrived(k, 2, b_out.at[k, t_of(0, 1 - core)])
        b_arrived(k, 5, b_out.at[k, t_of(-1, 1 - core)])
        b_arrived(k, 6, b_out.at[k, t_of(1, 1 - core)])
        b_arrived(k, 7, b_out.at[k, t_of(2, 1 - core), lower])
        b_arrived(k, 8, b_out.at[k, t_of(2, 1 - core), upper])

    first_hop(0)
    first_hop(1)
    first_hop(2)
    for u in range(UNITS + 1):
        if u < UNITS:
            second_hop(u)
            if u + 3 < UNITS:
                first_hop(u + 3)
        if u == 0:
            continue
        value = finish(u - 1)
        if u - 1 < SLOTS:
            send_second(u - 1, value)
        else:
            send_first(u - 1 - SLOTS, value)
        if 0 <= u - 2 < SLOTS:
            pass_second(u - 2)
        if 0 <= u - 3 < SLOTS:
            share_second(u - 3)
    for k in range(SLOTS):
        close_second(k)
        copies["o", k].wait()
    for k in range(SLOTS):
        for d in range(1, NTM):
            come = (t + NTM - d) % NTM
            pltpu.make_async_remote_copy(
                src_ref=packed.at[k, 0], dst_ref=p_out.at[come, k],
                send_sem=p_send.at[k, d], recv_sem=p_recv.at[k, d],
                device_id=sibling, device_id_type=MESH,
            ).wait_recv()
        copies["p", k, 0].wait()
    for copy in z_started:
        copy.wait_send()
    for u in range(UNITS):
        for s in (0, 1):
            for kind in ("a", "m"):
                copies[kind, u, s].wait_send()
    for k in range(SLOTS):
        for d in range(1, NTM):
            copies["p", k, d].wait_send()
        for n in range(9):
            copies["b", k, n].wait_send()


def exchange(traces, owner, tiles):
    seg_count = traces.shape[0]
    rows = seg_count * BLOCK
    tab_hi, tab_lo = forward_table()
    hbm = pl.BlockSpec(memory_space=pltpu.HBM)
    anywhere = pl.BlockSpec(memory_space=pl.ANY)
    half_units = (UNITS, 2, NG, 16, BLOCK)
    dma = pltpu.SemaphoreType.DMA
    return pl.pallas_call(
        exchange_kernel,
        out_shape=(
            jax.ShapeDtypeStruct((SLOTS, NTM, NG, 2, 16, BLOCK), BF),
            jax.ShapeDtypeStruct((NTM, SLOTS, 2, 16, 2 * NF), BF),
        ),
        in_specs=[hbm, hbm, hbm, hbm, hbm],
        out_specs=(anywhere, anywhere),
        scratch_shapes=[
            pltpu.SMEM(owner.shape, jnp.int32),
            pltpu.SMEM(tiles.shape[::-1], jnp.int32),
            pltpu.VMEM((rows, NT), F32),
            pltpu.VMEM((2 * NF, NT), BF),
            pltpu.VMEM((2 * NF, NT), BF),
            dma((6,)),
            pltpu.VMEM((NZ, 2, NG, 16, BLOCK), BF),
            pltpu.VMEM((SLOTS, NG, 2, 16, BLOCK), BF),
            pltpu.VMEM(half_units, BF),
            pltpu.VMEM(half_units, BF),
            pltpu.VMEM(half_units, BF),
            pltpu.VMEM(half_units, BF),
            pltpu.VMEM(half_units, BF),
            pltpu.VMEM(half_units, BF),
            pltpu.VMEM((SLOTS, NTM, 2, 16, 2 * NF), BF),
            pltpu.VMEM((NY, 8, 128), jnp.int32),
            pltpu.SMEM((NY, 8, 128), jnp.int32),
            dma((2, NZ // 2, CHUNKS)), dma((2, NZ // 2, CHUNKS)),
            dma((NY,)), dma((NY,)), dma((NY,)),
            dma((UNITS, 2)), dma((UNITS, 2)),
            dma((UNITS, 2)), dma((UNITS, 2)),
            dma((SLOTS, 9)), dma((SLOTS, 9)),
            dma((SLOTS, NTM)), dma((SLOTS, NTM)),
            dma((2 * SLOTS,)),
        ],
        compiler_params=pltpu.CompilerParams(
            collective_id=0, has_side_effects=True, vmem_limit_bytes=48 << 20
        ),
        name="exchange",
    )(*[in_hbm(a) for a in (traces.reshape(rows, NT), tab_hi, tab_lo, owner, tiles.T)])


def stack_kernel(
    scale, counts, p_ref, b_ref, hi_hbm, lo_hbm, out,
    inv_hi, inv_lo, natural, first, turned, high, low, result, load_sem, out_sem,
):
    loads = [
        pltpu.make_async_copy(hi_hbm, inv_hi, load_sem.at[0]),
        pltpu.make_async_copy(lo_hbm, inv_lo, load_sem.at[1]),
    ]
    for load in loads:
        load.start()

    eye = identity(2 * NF)
    used = SLOTS * 32
    pad = jnp.zeros((2 * NF, BLOCK - used), BF)
    for t in range(NTM):
        back = nt_dot(eye, p_ref[t].reshape(used, 2 * NF)).astype(BF)
        natural[t] = jnp.concatenate([back, pad], axis=1)
    eye = identity(BLOCK)
    for g in range(NG):
        tile = natural[:, g * 16 : (g + 1) * 16, :]
        first[g] = nt_dot(eye, tile.reshape(BLOCK, BLOCK))
        wide = tile.astype(F32)
        wide = jnp.concatenate([-wide[:, 8:], wide[:, :8]], axis=1)
        turned[g] = nt_dot(eye, wide.astype(BF).reshape(BLOCK, BLOCK))

    shape = (8, BLOCK)
    mask = lax.broadcasted_iota(jnp.int32, shape, 1) % 8 == lax.broadcasted_iota(
        jnp.int32, shape, 0
    )
    mask = jnp.where(mask, 1.0, 0.0).astype(F32)[None]

    def group(k, g):
        halves = []
        for s in (0, 1):
            rows = slice(k * 32 + s * 16, k * 32 + s * 16 + 16)
            direct = first[g, rows, :][:, None, :] * mask
            crossed = turned[g, rows, :][:, None, :] * mask
            both = jnp.concatenate([direct, crossed], axis=1).astype(BF)
            halves.append(both.reshape(2 * NF, BLOCK))
        lhs = jnp.concatenate(halves, axis=1)
        rhs = jnp.concatenate([b_ref[k, t, g, s] for s in (0, 1) for t in range(NTM)], axis=0)
        cross = jnp.dot(lhs, rhs, preferred_element_type=F32).reshape(16, 16, BLOCK)
        rows = slice(g * 16, g * 16 + 16)
        top = cross.astype(BF)
        high[k, :, rows, :] = top
        low[k, :, rows, :] = (cross - top.astype(F32)).astype(BF)

    copies = []
    for k in range(SLOTS):
        for g in range(NG):
            group(k, g)
        if k == 0:
            for load in loads:
                load.wait()
        factor = jnp.where(k < counts[0], scale, 0.0)
        for i in range(0, 16, 2):
            c_hi = jnp.concatenate([high[k, i], high[k, i + 1]], axis=1)
            c_lo = jnp.concatenate([low[k, i], low[k, i + 1]], axis=1)
            lagged = jnp.dot(inv_hi[...], c_hi, preferred_element_type=F32)
            lagged = lagged + jnp.dot(inv_lo[...], c_hi, preferred_element_type=F32)
            lagged = lagged + jnp.dot(inv_hi[...], c_lo, preferred_element_type=F32)
            result[k, :, i * BLOCK : (i + 2) * BLOCK] = lagged * factor
            if i % 8 == 6:
                lanes = pl.ds((i - 6) * BLOCK, 8 * BLOCK)
                copy = pltpu.make_async_copy(
                    result.at[k, :, lanes], out.at[k, :, lanes], out_sem.at[k, i // 8]
                )
                copy.start()
                copies.append(copy)
    for copy in copies:
        copy.wait()


def stack(counts, p_all, b_all, scale):
    inv_hi, inv_lo = inverse_table()
    share = BLOCK // NTM
    vmem = pl.BlockSpec(memory_space=pltpu.VMEM)
    hbm = pl.BlockSpec(memory_space=pltpu.HBM)
    return pl.pallas_call(
        functools.partial(stack_kernel, scale),
        out_shape=jax.ShapeDtypeStruct((SLOTS, LAGS, share * BLOCK), F32),
        in_specs=[pl.BlockSpec(memory_space=pltpu.SMEM), vmem, vmem, hbm, hbm],
        out_specs=hbm,
        scratch_shapes=[
            pltpu.VMEM((LAGS, 2 * NF), BF),
            pltpu.VMEM((LAGS, 2 * NF), BF),
            pltpu.VMEM((NTM, 2 * NF, BLOCK), BF),
            pltpu.VMEM((NG, BLOCK, BLOCK), F32),
            pltpu.VMEM((NG, BLOCK, BLOCK), F32),
            pltpu.VMEM((SLOTS, 16, 2 * NF, BLOCK), BF),
            pltpu.VMEM((SLOTS, 16, 2 * NF, BLOCK), BF),
            pltpu.VMEM((SLOTS, LAGS, share * BLOCK), F32),
            pltpu.SemaphoreType.DMA((2,)),
            pltpu.SemaphoreType.DMA((SLOTS, 2)),
        ],
        compiler_params=pltpu.CompilerParams(vmem_limit_bytes=32 << 20),
        name="stack",
    )(counts, p_all, b_all, in_hbm(inv_hi), in_hbm(inv_lo))


def shards(traces, owner, tiles, counts):
    segments = traces.shape[0] * NTM
    b_all, p_all = exchange(traces, owner, tiles)
    return stack(counts, p_all, b_all, 1.0 / math.sqrt(segments * NF))


def solution(mesh):
    placed = (P("tm", "pair", None), P(), P("pair", None), P("pair"))
    return jax.shard_map(
        shards, mesh=mesh, in_specs=placed, out_specs=P("pair", None, "tm"), check_vma=False
    )
```

```python
import functools
import math

import jax
import jax.numpy as jnp
import ml_dtypes
import numpy as np
from jax import lax
from jax.experimental import pallas as pl
from jax.experimental.pallas import tpu as pltpu
from jax.sharding import PartitionSpec as P

BLOCK = 128
NT = 1024
NF = 128
LOW_BIN = 8
LAGS = 128
NG = 16
NZ = 16
NY = 4
NX = 4
NTM = 8
SLOTS = 3
UNITS = 2 * SLOTS
CHUNKS = 8
GC = 2 * NG // CHUNKS
BF = jnp.bfloat16
F32 = jnp.float32
MESH = pl.DeviceIdType.MESH


def split(table):
    high = table.astype(np.float32).astype(ml_dtypes.bfloat16)
    low = (table.astype(np.float32) - high.astype(np.float32)).astype(ml_dtypes.bfloat16)
    return high, low


def forward_table():
    samples = np.arange(NT)
    bins = LOW_BIN + np.arange(NF)
    angle = (bins[:, None] * samples[None, :] % NT) * (2.0 * math.pi / NT)
    return split(np.concatenate([np.cos(angle), -np.sin(angle)], axis=0))


def inverse_table():
    shifts = np.arange(LAGS) - LAGS // 2
    bins = LOW_BIN + np.arange(NF)
    angle = (shifts[:, None] * bins[None, :] % NT) * (2.0 * math.pi / NT)
    parts = np.stack([np.cos(angle), -np.sin(angle)], axis=0)
    parts = parts.reshape(2, LAGS, NG, 8).transpose(1, 2, 0, 3)
    return split(parts.reshape(LAGS, 2 * NF))


def in_hbm(array):
    return pltpu.with_memory_space_constraint(jnp.asarray(array), pltpu.HBM)


def nt_dot(a, b):
    return lax.dot_general(a, b, (((1,), (1,)), ((), ())), preferred_element_type=F32)


def identity(size):
    row = lax.broadcasted_iota(jnp.int32, (size, size), 0)
    return jnp.where(row == lax.broadcasted_iota(jnp.int32, (size, size), 1), 1.0, 0.0).astype(BF)


def exchange_kernel(
    traces_hbm, hi_hbm, lo_hbm, owner_hbm, tiles_hbm, b_out, p_out,
    owner, tiles, traces, tab_hi, tab_lo, load_sem, slabs, picks, stage_a, stage_d, stage_m, got_x, got_p, got_m,
    packed, req_v, req_s,
    z_send, z_recv, r_send, r_recv, r_loc, a_send, a_recv, d_send, d_recv, m_send, m_recv,
    b_send, b_recv, p_send, p_recv, own_sem,
):
    t = lax.axis_index("tm")
    pair = lax.axis_index("pair")
    z, y = pair // NY, pair % NY
    x, core = t // 2, t % 2

    def at_z(step):
        return {"pair": ((z + step + NZ) % NZ) * NY + y}

    def at_y(step):
        return {"pair": z * NY + (y + step + NY) % NY}

    def at_x(step):
        return {"tm": ((x + step + NX) % NX) * 2 + core}

    def at_t(step):
        return {"tm": (t + step) % NTM}

    sibling = {"tm": x * 2 + 1 - core}

    barrier = pltpu.get_barrier_semaphore()
    greet = [at_z(1), at_z(-1)] + [at_y(d) for d in (1, 2, 3)] + [at_t(d) for d in range(1, NTM)]
    for who in greet:
        pl.semaphore_signal(barrier, inc=1, device_id=who, device_id_type=MESH)

    def load(n, src, dst):
        copy = pltpu.make_async_copy(src, dst, load_sem.at[n])
        copy.start()
        return copy

    rows = [pl.ds(seg * BLOCK, BLOCK) for seg in (0, 1)]
    early = [
        load(0, owner_hbm, owner), load(1, tiles_hbm, tiles),
        load(2, traces_hbm.at[rows[0]], traces.at[rows[0]]),
        load(3, hi_hbm, tab_hi), load(4, lo_hbm, tab_lo),
    ]
    late = load(5, traces_hbm.at[rows[1]], traces.at[rows[1]])
    for copy in early:
        copy.wait()

    def transform(seg):
        values = traces[rows[seg], :]
        v_hi = values.astype(BF)
        v_lo = (values - v_hi.astype(F32)).astype(BF)
        spec = nt_dot(tab_hi[...], v_hi) + (nt_dot(tab_hi[...], v_lo) + nt_dot(tab_lo[...], v_hi))
        real, imag = spec[:NF], spec[NF:]
        power = real * real + imag * imag
        bin_of = lax.broadcasted_iota(jnp.int32, power.shape, 0)
        total = power
        for step in (1, 2):
            ahead = pltpu.roll(power, NF - step, 0)
            behind = pltpu.roll(power, step, 0)
            total = total + jnp.where(bin_of < NF - step, ahead, 0.0)
            total = total + jnp.where(bin_of >= step, behind, 0.0)
        edge = jnp.minimum(jnp.minimum(bin_of, NF - 1 - bin_of), 2)
        smooth = total / (edge + 3).astype(F32)
        level = jnp.sum(power, axis=0, keepdims=True) * (1.0 / NF)
        factor = lax.rsqrt(smooth + 0.05 * level + 1e-06)
        slabs[z, seg] = jnp.concatenate(
            [(real * factor).reshape(NG, 8, BLOCK), (imag * factor).reshape(NG, 8, BLOCK)], axis=1
        ).astype(BF)

    transform(0)

    mine = []
    lane = lax.broadcasted_iota(jnp.int32, (8, 128), 1)
    row = jnp.zeros((8, 128), jnp.int32)
    for u in range(UNITS):
        wanted = owner[tiles[1 - u // SLOTS, u % SLOTS]]
        mine.append(wanted)
        row = jnp.where(lane == u, wanted, row)
    req_v[0] = row

    pl.semaphore_wait(barrier, len(greet))

    def z_copy(way, step, c):
        sign = 1 - 2 * way
        index = (z - sign * step + NZ) % NZ
        ref = slabs.at[index, c * GC // NG, pl.ds(c * GC % NG, GC)]
        return pltpu.make_async_remote_copy(
            src_ref=ref, dst_ref=ref,
            send_sem=z_send.at[way, step, c], recv_sem=z_recv.at[way, step, c],
            device_id=at_z(sign), device_id_type=MESH,
        )

    def z_arrived(way, step, c):
        sign = 1 - 2 * way
        index = (z - sign * (step + 1) + NZ) % NZ
        ref = slabs.at[index, c * GC // NG, pl.ds(c * GC % NG, GC)]
        pltpu.make_async_remote_copy(
            src_ref=ref, dst_ref=ref,
            send_sem=z_send.at[way, step, c], recv_sem=z_recv.at[way, step, c],
            device_id=at_z(sign), device_id_type=MESH,
        ).wait_recv()

    last = NZ // 2 - 1

    def z_pieces(step):
        for c in range(CHUNKS):
            for way in (0, 1):
                if step < last or (c < CHUNKS // 2) == (way == 0):
                    yield way, c

    z_started = []
    for way, c in z_pieces(0):
        if (way, c) == (0, CHUNKS // 2):
            late.wait()
            transform(1)
        copy = z_copy(way, 0, c)
        copy.start()
        z_started.append(copy)

    r_copies = []
    for d in (1, 2, 3):
        copy = pltpu.make_async_remote_copy(
            src_ref=req_v.at[0], dst_ref=req_v.at[d],
            send_sem=r_send.at[d], recv_sem=r_recv.at[d],
            device_id=at_y(d), device_id_type=MESH,
        )
        copy.start()
        r_copies.append(copy)

    def fetch_requests():
        for copy in r_copies:
            copy.wait()
        local = [
            pltpu.make_async_copy(req_v.at[d], req_s.at[d], r_loc.at[d]) for d in (1, 2, 3)
        ]
        for copy in local:
            copy.start()
        for copy in local:
            copy.wait()

    for step in range(1, last + 1):
        for way, c in z_pieces(step):
            z_arrived(way, step - 1, c)
            copy = z_copy(way, step, c)
            copy.start()
            z_started.append(copy)
        if step == 4:
            fetch_requests()
        if step == last:
            for c in range(CHUNKS):
                for way in (0, 1):
                    if (way, c) not in list(z_pieces(last)):
                        z_arrived(way, step - 1, c)
    for way, c in z_pieces(last):
        z_arrived(way, last, c)

    def asked(d, u):
        wanted = mine[u] if d == 0 else req_s[(NY - d) % NY, 0, u]
        return wanted // NY, wanted % NY

    def send(src, dst, s_sem, r_sem, who):
        copy = pltpu.make_async_remote_copy(
            src_ref=src, dst_ref=dst, send_sem=s_sem, recv_sem=r_sem,
            device_id=who, device_id_type=MESH,
        )
        copy.start()
        return copy

    copies = {}
    eye = identity(BLOCK)

    def first_hop(u):
        index, _ = asked(2, u)
        for s in (0, 1):
            stage_a[u, s] = slabs[index, s]
            copies["a", u, s] = send(
                stage_a.at[u, s], got_x.at[u, s], a_send.at[u, s], a_recv.at[u, s],
                at_y(1 if s == 0 else -1),
            )

    def direct(u):
        for s, d, got in ((1, 1, got_p), (0, -1, got_m)):
            index, _ = asked(d % NY, u)
            stage_d[u, s] = slabs[index, s]
            copies["d", u, s] = send(
                stage_d.at[u, s], got.at[u, s], d_send.at[u, s], d_recv.at[u, s], at_y(d)
            )

    def merged(u):
        for s, d, got in ((0, 1, got_p), (1, -1, got_m)):
            index, column = asked(d % NY, u)
            copies["a", u, s].wait_recv()
            stage_m[u, s] = jnp.where(column == y, slabs[index, s], got_x[u, s])
            copies["m", u, s] = send(
                stage_m.at[u, s], got.at[u, s], m_send.at[u, s], m_recv.at[u, s], at_y(d)
            )

    def finish(u):
        index, column = asked(0, u)
        for s in (0, 1):
            copies["d", u, s].wait_recv()
            copies["m", u, s].wait_recv()
        up, down = (y + 1) % NY, (y + NY - 1) % NY
        own = column == y
        low = jnp.where(column == up, got_m[u, 0], got_p[u, 0])
        low = jnp.where(own, slabs[index, 0], low)
        high = jnp.where(column == down, got_p[u, 1], got_m[u, 1])
        high = jnp.where(own, slabs[index, 1], high)
        return low, high

    def send_first(k, value):
        for seg in (0, 1):
            turned = nt_dot(eye, value[seg].reshape(2 * NF, BLOCK)).astype(BF)
            packed[k, :, seg] = turned.reshape(NTM, 16, 2 * NF)
        for d in range(1, NTM):
            to = (t + d) % NTM
            copies["p", k, d] = send(
                packed.at[k, to], p_out.at[t, k], p_send.at[k, d], p_recv.at[k, d], at_t(d)
            )
        copies["p", k, 0] = pltpu.make_async_copy(
            packed.at[k, t], p_out.at[t, k], own_sem.at[SLOTS + k]
        )
        copies["p", k, 0].start()

    half = NG // 2

    def t_of(step, c=None):
        return ((x + step + NX) % NX) * 2 + (core if c is None else c)

    def b_send_to(k, n, src, where, who):
        copies["b", k, n] = send(src, where, b_send.at[k, n], b_recv.at[k, n], who)

    def b_arrived(k, n, ref):
        pltpu.make_async_remote_copy(
            src_ref=ref, dst_ref=ref, send_sem=b_send.at[k, n], recv_sem=b_recv.at[k, n],
            device_id=sibling, device_id_type=MESH,
        ).wait_recv()

    def send_second(k, value):
        picks[k, :, 0], picks[k, :, 1] = value
        mine_ref = picks.at[k]
        b_send_to(k, 0, mine_ref, b_out.at[k, t], at_x(1))
        b_send_to(k, 1, mine_ref, b_out.at[k, t], at_x(-1))
        b_send_to(k, 2, mine_ref, b_out.at[k, t], sibling)
        copies["o", k] = pltpu.make_async_copy(mine_ref, b_out.at[k, t], own_sem.at[k])
        copies["o", k].start()

    lower, upper = pl.ds(0, half), pl.ds(half, half)

    def pass_second(k):
        low = b_out.at[k, t_of(-1)]
        b_arrived(k, 0, low)
        b_send_to(k, 3, b_out.at[k, t_of(-1), lower], b_out.at[k, t_of(-1), lower], at_x(1))
        b_send_to(k, 5, low, low, sibling)
        high = b_out.at[k, t_of(1)]
        b_arrived(k, 1, high)
        b_send_to(k, 4, b_out.at[k, t_of(1), upper], b_out.at[k, t_of(1), upper], at_x(-1))
        b_send_to(k, 6, high, high, sibling)

    def share_second(k):
        far_low = b_out.at[k, t_of(2), lower]
        b_arrived(k, 3, far_low)
        b_send_to(k, 7, far_low, far_low, sibling)
        far_up = b_out.at[k, t_of(2), upper]
        b_arrived(k, 4, far_up)
        b_send_to(k, 8, far_up, far_up, sibling)

    def close_second(k):
        b_arrived(k, 2, b_out.at[k, t_of(0, 1 - core)])
        b_arrived(k, 5, b_out.at[k, t_of(-1, 1 - core)])
        b_arrived(k, 6, b_out.at[k, t_of(1, 1 - core)])
        b_arrived(k, 7, b_out.at[k, t_of(2, 1 - core), lower])
        b_arrived(k, 8, b_out.at[k, t_of(2, 1 - core), upper])

    first_hop(0)
    first_hop(1)
    direct(0)
    for u in range(UNITS + 1):
        if u < UNITS:
            merged(u)
            if u + 2 < UNITS:
                first_hop(u + 2)
            if u + 1 < UNITS:
                direct(u + 1)
        if u == 0:
            continue
        value = finish(u - 1)
        if u - 1 < SLOTS:
            send_second(u - 1, value)
        else:
            send_first(u - 1 - SLOTS, value)
        if 0 <= u - 2 < SLOTS:
            pass_second(u - 2)
        if 0 <= u - 3 < SLOTS:
            share_second(u - 3)
    for k in range(SLOTS):
        close_second(k)
        copies["o", k].wait()
    for k in range(SLOTS):
        for d in range(1, NTM):
            come = (t + NTM - d) % NTM
            pltpu.make_async_remote_copy(
                src_ref=packed.at[k, 0], dst_ref=p_out.at[come, k],
                send_sem=p_send.at[k, d], recv_sem=p_recv.at[k, d],
                device_id=sibling, device_id_type=MESH,
            ).wait_recv()
        copies["p", k, 0].wait()
    for copy in z_started:
        copy.wait_send()
    for u in range(UNITS):
        for s in (0, 1):
            for kind in ("a", "d", "m"):
                copies[kind, u, s].wait_send()
    for k in range(SLOTS):
        for d in range(1, NTM):
            copies["p", k, d].wait_send()
        for n in range(9):
            copies["b", k, n].wait_send()


def exchange(traces, owner, tiles):
    seg_count = traces.shape[0]
    rows = seg_count * BLOCK
    tab_hi, tab_lo = forward_table()
    hbm = pl.BlockSpec(memory_space=pltpu.HBM)
    anywhere = pl.BlockSpec(memory_space=pl.ANY)
    half_units = (UNITS, 2, NG, 16, BLOCK)
    dma = pltpu.SemaphoreType.DMA
    return pl.pallas_call(
        exchange_kernel,
        out_shape=(
            jax.ShapeDtypeStruct((SLOTS, NTM, NG, 2, 16, BLOCK), BF),
            jax.ShapeDtypeStruct((NTM, SLOTS, 2, 16, 2 * NF), BF),
        ),
        in_specs=[hbm, hbm, hbm, hbm, hbm],
        out_specs=(anywhere, anywhere),
        scratch_shapes=[
            pltpu.SMEM(owner.shape, jnp.int32),
            pltpu.SMEM(tiles.shape[::-1], jnp.int32),
            pltpu.VMEM((rows, NT), F32),
            pltpu.VMEM((2 * NF, NT), BF),
            pltpu.VMEM((2 * NF, NT), BF),
            dma((6,)),
            pltpu.VMEM((NZ, 2, NG, 16, BLOCK), BF),
            pltpu.VMEM((SLOTS, NG, 2, 16, BLOCK), BF),
            pltpu.VMEM(half_units, BF),
            pltpu.VMEM(half_units, BF),
            pltpu.VMEM(half_units, BF),
            pltpu.VMEM(half_units, BF),
            pltpu.VMEM(half_units, BF),
            pltpu.VMEM(half_units, BF),
            pltpu.VMEM((SLOTS, NTM, 2, 16, 2 * NF), BF),
            pltpu.VMEM((NY, 8, 128), jnp.int32),
            pltpu.SMEM((NY, 8, 128), jnp.int32),
            dma((2, NZ // 2, CHUNKS)), dma((2, NZ // 2, CHUNKS)),
            dma((NY,)), dma((NY,)), dma((NY,)),
            dma((UNITS, 2)), dma((UNITS, 2)),
            dma((UNITS, 2)), dma((UNITS, 2)),
            dma((UNITS, 2)), dma((UNITS, 2)),
            dma((SLOTS, 9)), dma((SLOTS, 9)),
            dma((SLOTS, NTM)), dma((SLOTS, NTM)),
            dma((2 * SLOTS,)),
        ],
        compiler_params=pltpu.CompilerParams(
            collective_id=0, has_side_effects=True, vmem_limit_bytes=48 << 20
        ),
        name="exchange",
    )(*[in_hbm(a) for a in (traces.reshape(rows, NT), tab_hi, tab_lo, owner, tiles.T)])


def stack_kernel(
    scale, counts, p_ref, b_ref, hi_hbm, lo_hbm, out,
    inv_hi, inv_lo, natural, first, turned, high, low, result, load_sem, out_sem,
):
    loads = [
        pltpu.make_async_copy(hi_hbm, inv_hi, load_sem.at[0]),
        pltpu.make_async_copy(lo_hbm, inv_lo, load_sem.at[1]),
    ]
    for load in loads:
        load.start()

    eye = identity(2 * NF)
    used = SLOTS * 32
    pad = jnp.zeros((2 * NF, BLOCK - used), BF)
    for t in range(NTM):
        back = nt_dot(eye, p_ref[t].reshape(used, 2 * NF)).astype(BF)
        natural[t] = jnp.concatenate([back, pad], axis=1)
    eye = identity(BLOCK)
    for g in range(NG):
        tile = natural[:, g * 16 : (g + 1) * 16, :]
        first[g] = nt_dot(eye, tile.reshape(BLOCK, BLOCK))
        wide = tile.astype(F32)
        wide = jnp.concatenate([-wide[:, 8:], wide[:, :8]], axis=1)
        turned[g] = nt_dot(eye, wide.astype(BF).reshape(BLOCK, BLOCK))

    shape = (8, BLOCK)
    mask = lax.broadcasted_iota(jnp.int32, shape, 1) % 8 == lax.broadcasted_iota(
        jnp.int32, shape, 0
    )
    mask = jnp.where(mask, 1.0, 0.0).astype(F32)[None]

    def group(k, g):
        halves = []
        for s in (0, 1):
            rows = slice(k * 32 + s * 16, k * 32 + s * 16 + 16)
            direct = first[g, rows, :][:, None, :] * mask
            crossed = turned[g, rows, :][:, None, :] * mask
            both = jnp.concatenate([direct, crossed], axis=1).astype(BF)
            halves.append(both.reshape(2 * NF, BLOCK))
        lhs = jnp.concatenate(halves, axis=1)
        rhs = jnp.concatenate([b_ref[k, t, g, s] for s in (0, 1) for t in range(NTM)], axis=0)
        cross = jnp.dot(lhs, rhs, preferred_element_type=F32).reshape(16, 16, BLOCK)
        rows = slice(g * 16, g * 16 + 16)
        top = cross.astype(BF)
        high[k, :, rows, :] = top
        low[k, :, rows, :] = (cross - top.astype(F32)).astype(BF)

    copies = []
    for k in range(SLOTS):
        for g in range(NG):
            group(k, g)
        if k == 0:
            for load in loads:
                load.wait()
        factor = jnp.where(k < counts[0], scale, 0.0)
        for i in range(0, 16, 2):
            c_hi = jnp.concatenate([high[k, i], high[k, i + 1]], axis=1)
            c_lo = jnp.concatenate([low[k, i], low[k, i + 1]], axis=1)
            lagged = jnp.dot(inv_hi[...], c_hi, preferred_element_type=F32)
            lagged = lagged + jnp.dot(inv_lo[...], c_hi, preferred_element_type=F32)
            lagged = lagged + jnp.dot(inv_hi[...], c_lo, preferred_element_type=F32)
            result[k, :, i * BLOCK : (i + 2) * BLOCK] = lagged * factor
            if i % 8 == 6:
                lanes = pl.ds((i - 6) * BLOCK, 8 * BLOCK)
                copy = pltpu.make_async_copy(
                    result.at[k, :, lanes], out.at[k, :, lanes], out_sem.at[k, i // 8]
                )
                copy.start()
                copies.append(copy)
    for copy in copies:
        copy.wait()


def stack(counts, p_all, b_all, scale):
    inv_hi, inv_lo = inverse_table()
    share = BLOCK // NTM
    vmem = pl.BlockSpec(memory_space=pltpu.VMEM)
    hbm = pl.BlockSpec(memory_space=pltpu.HBM)
    return pl.pallas_call(
        functools.partial(stack_kernel, scale),
        out_shape=jax.ShapeDtypeStruct((SLOTS, LAGS, share * BLOCK), F32),
        in_specs=[pl.BlockSpec(memory_space=pltpu.SMEM), vmem, vmem, hbm, hbm],
        out_specs=hbm,
        scratch_shapes=[
            pltpu.VMEM((LAGS, 2 * NF), BF),
            pltpu.VMEM((LAGS, 2 * NF), BF),
            pltpu.VMEM((NTM, 2 * NF, BLOCK), BF),
            pltpu.VMEM((NG, BLOCK, BLOCK), F32),
            pltpu.VMEM((NG, BLOCK, BLOCK), F32),
            pltpu.VMEM((SLOTS, 16, 2 * NF, BLOCK), BF),
            pltpu.VMEM((SLOTS, 16, 2 * NF, BLOCK), BF),
            pltpu.VMEM((SLOTS, LAGS, share * BLOCK), F32),
            pltpu.SemaphoreType.DMA((2,)),
            pltpu.SemaphoreType.DMA((SLOTS, 2)),
        ],
        compiler_params=pltpu.CompilerParams(vmem_limit_bytes=32 << 20),
        name="stack",
    )(counts, p_all, b_all, in_hbm(inv_hi), in_hbm(inv_lo))


def shards(traces, owner, tiles, counts):
    segments = traces.shape[0] * NTM
    b_all, p_all = exchange(traces, owner, tiles)
    return stack(counts, p_all, b_all, 1.0 / math.sqrt(segments * NF))


def solution(mesh):
    placed = (P("tm", "pair", None), P(), P("pair", None), P("pair"))
    return jax.shard_map(
        shards, mesh=mesh, in_specs=placed, out_specs=P("pair", None, "tm"), check_vma=False
    )
```
